256 devices in a mesh: seq: 32 (over z_hi, x, core), tensor: 8 (over y, z_lo).
Axes of the slice: x: 4, y: 4, z: 8 (z_hi: 4, z_lo: 2; z = z_hi * 2 + z_lo), core: 2. Of those that a mesh axis runs over, the one named last changes fastest.
Arguments:
- tokens: bfloat16 [4096, 2048], P('seq'), may hold values from -6 to 6
- lengths: int32 [8], replicated, may hold values from 1 to 2048, 4096 in all
- page_table: int32 [256], replicated, may hold values from 0 to 255, each once
- attention_gain: float32 [2048], replicated, may hold values from 0.25 to 1.75
- query_weight: bfloat16 [2048, 2048], P(None, 'tensor')
- key_weight: bfloat16 [2048, 2048], P(None, 'tensor')
- value_weight: bfloat16 [2048, 2048], P(None, 'tensor'), may hold values from -0.125 to 0.125
- out_weight: bfloat16 [2048, 2048], P('tensor'), may hold values from -0.125 to 0.125
- expert_gain: float32 [2048], replicated, may hold values from 0.25 to 1.75
- router_weight: bfloat16 [2048, 64], replicated, may hold values from -0.03125 to 0.03125
- expert_ids: int32 [4096, 8], P('seq'), may hold values from 0 to 63, all different within a row; in each aligned block of 128 rows (0 to 127, 128 to 255, ...) at most 24 rows name the same one
- gate_weight: bfloat16 [64, 2048, 1024], P('seq', None, 'tensor'), may hold values from -0.125 to 0.125
- up_weight: bfloat16 [64, 2048, 1024], P('seq', None, 'tensor'), may hold values from -0.125 to 0.125
- down_weight: bfloat16 [64, 1024, 2048], P('seq', 'tensor'), may hold values from -6 to 6
Outputs:
- layer_out: bfloat16 [4096, 2048], P('seq')
- key_cache: bfloat16 [256, 16, 2048], P('seq', None, 'tensor')
- value_cache: bfloat16 [256, 16, 2048], P('seq', None, 'tensor')
The draws below stay inside these ranges and needn't reach their ends.
Inputs may be any that keep to these rules, and one draw needn't show every extreme that they name: The 8 lengths sum to 4096; the longest is exactly 2048. `page_table`: every page number appears once. `expert_ids`: each token names 8 different experts; among the 128 tokens of one index of seq no expert is named more than 24 times, a bound that some block reaches.
All inputs are finite; a program needn't handle non-finite values.
Results may differ from the reference program's by a relative error of at most 0.023.
Values may be sent and summed in bfloat16 or wider, within the bound.
A program may use at most 128 MiB of HBM per device.

```python
import math
import jax
import jax.numpy as jnp
import numpy as np
from jax import lax

D = 2048
HEADS = 16
HEAD_DIM = 128
FF = 1024
TOPK = 8
EXPERTS = 64
TOK_DEV = 128
TOKENS = 4096
SEGS = 8
MAXLEN = 2048
PAGE = 16
PAGES = 256
CAP = 24
N_SEQ = 32
N_TENSOR = 8


def draw_query_weight(key, part):
    own_part = jax.random.normal(jax.random.fold_in(key, 7), (D, HEADS * HEAD_DIM), jnp.float32)
    return (own_part * D ** (-0.5)).astype(jnp.bfloat16)


def draw_key_weight(key, part):
    own_part = jax.random.normal(jax.random.fold_in(key, 9), (D, HEADS * HEAD_DIM), jnp.float32)
    return (own_part * D ** (-0.5)).astype(jnp.bfloat16)


def shard_levels(key, shape, cuts, low, top_value):
    def one(axis_at, parts):
        steps = jax.random.uniform(jax.random.fold_in(jax.random.fold_in(key, 6), axis_at), (parts,), jnp.float32, low / len(cuts), top_value / len(cuts))
        return jnp.repeat(jnp.exp(steps), shape[axis_at] // parts).reshape((-1,) + (1,) * (len(shape) - axis_at - 1))

    gain = one(*cuts[0])
    for cut in cuts[1:]:
        gain = gain * one(*cut)
    return gain


def length_profile(number_of, total, limit, slope):
    loads = [(1 << 20) // math.isqrt(standing ** slope) + 1 for standing in range(2, number_of + 1)]
    spare, holding = total - limit - (number_of - 1), [1] * (number_of - 1)
    while spare > 0:
        movable = [i for i in range(number_of - 1) if holding[i] < limit]
        whole, left = sum([loads[i] for i in movable]), spare
        for i in movable:
            addition = min(limit - holding[i], max(1, left * loads[i] // whole), spare)
            holding[i] = holding[i] + addition
            spare = spare - addition
    return np.array([limit] + holding)


def uneven(key, number_of, total, bound, slope):
    if number_of == 2:
        one = jax.random.randint(key, (), max(1, total - bound), min(bound, total - 1) + 1)
        return jnp.stack([one, total - one])
    tallies = jnp.asarray(length_profile(number_of, total, bound, slope), jnp.int32)
    pairs = (number_of - 1) // 2
    giver, sink = tallies[1:1 + 2 * pairs:2], tallies[2:2 + 2 * pairs:2]
    slack = jnp.minimum(giver - 1, bound - sink)
    passed = jax.random.randint(jax.random.fold_in(key, 1), (pairs,), 0, 1 << 20) % (slack + 1)
    tallies = tallies.at[1:1 + 2 * pairs:2].set(giver - passed).at[2:2 + 2 * pairs:2].set(sink + passed)
    return tallies[jax.random.permutation(jax.random.fold_in(key, 2), number_of)]


def deal_out(own_key, own, number, rows, amount, top, most, lean):
    ranking = jax.random.permutation(own_key, amount)
    heavy_load, usual = portions_of(amount, rows * top, most, lean, True), portions_of(amount, rows * top, most, lean, False)
    places = jnp.arange(amount)

    def named(tallies, offset_by):
        used = int((tallies > 0).sum())
        fixed = max(1, used // 4)
        moved = fixed + (places - fixed + offset_by * (used - fixed)) % max(1, amount - fixed)
        return jnp.zeros((amount,), jnp.int32).at[ranking[jnp.where(places < fixed, places, moved)]].set(jnp.asarray(tallies, jnp.int32))

    tallies = jnp.where(number % 4 == 0, named(heavy_load, number // 4), named(usual, number - number // 4 - 1))
    mixed = jax.random.permutation(jax.random.fold_in(own, 3), amount)
    giver, receiver = mixed[0:amount // 2 * 2:2], mixed[1:amount // 2 * 2:2]
    room = jnp.minimum(tallies[giver] - 1, most - tallies[receiver]) // 2
    room = jnp.where((giver == ranking[0]) | (receiver == ranking[0]) | (tallies[receiver] == 0), 0, jnp.maximum(room, 0))
    moved = jax.random.randint(jax.random.fold_in(own, 4), (amount // 2,), 0, 1 << 20) % (room + 1)
    tallies = tallies.at[giver].add(-moved).at[receiver].add(moved)
    members = jnp.searchsorted(jnp.cumsum(tallies), jnp.arange(rows * top), side="right").astype(jnp.int32)
    listing = members.reshape(top, rows).T
    listing = listing[jax.random.permutation(jax.random.fold_in(own, 1), rows)]
    offset_by = jax.random.randint(jax.random.fold_in(own, 2), (rows, 1), 0, top)
    return jnp.take_along_axis(listing, (jnp.arange(top)[None, :] + offset_by) % top, axis=1)


def portions_of(number_of, total, most, slope, full):
    loads = [(1 << 20) // math.isqrt(rank ** slope) + 1 for rank in range(1, number_of + 1)]
    largest = most if full else min(most, max(-(-total // number_of), total * loads[0] // sum(loads)))
    least = 1 if total - largest >= number_of - 1 else 0
    counts, spare = [largest] + [least] * (number_of - 1), total - largest - least * (number_of - 1)
    while spare > 0:
        candidates = [i for i in range(1, number_of) if counts[i] < largest] or [i for i in range(1, number_of) if counts[i] < most]
        pool, remaining = sum([loads[i] for i in candidates]), spare
        for i in candidates:
            extra = min(most - counts[i], max(1, remaining * loads[i] // pool), spare)
            counts[i] = counts[i] + extra
            spare = spare - extra
    return np.array(counts)


def scatter_about(own_key, dims, deviation, bound, cuts=(), kind=jnp.bfloat16):
    values = deviation * jax.random.normal(own_key, dims, jnp.float32)
    if cuts:
        values = values * shard_levels(own_key, dims, cuts, -0.22, 0.18)
    return jnp.clip(values, -bound, bound).astype(kind)


def setup_inputs(seed: int = 0) -> dict:
    key_list = jax.random.split(jax.random.key(seed), 15)
    tokens = scatter_about(key_list[0], (TOKENS, D), 1.0, 6.0, ((0, 32),))
    lengths = uneven(key_list[1], SEGS, TOKENS, MAXLEN, 2).astype(jnp.int32)
    page_table = jax.random.permutation(key_list[2], PAGES).astype(jnp.int32)
    attention_gain = jnp.clip(1.0 + 0.15 * jax.random.normal(key_list[3], (D,), jnp.float32), 0.25, 1.75)
    query_weight = draw_query_weight(jax.random.fold_in(key_list[14], 71), 0)
    key_weight = draw_key_weight(jax.random.fold_in(key_list[14], 71), 0)
    value_weight = scatter_about(key_list[6], (D, HEADS * HEAD_DIM), D ** -0.5, 0.125, ((1, 8),))
    out_weight = scatter_about(key_list[7], (HEADS * HEAD_DIM, D), (HEADS * HEAD_DIM) ** -0.5, 0.125, ((0, 8),))
    expert_gain = jnp.clip(1.0 + 0.15 * jax.random.normal(key_list[8], (D,), jnp.float32), 0.25, 1.75)
    router_weight = scatter_about(key_list[9], (D, EXPERTS), (16 * D) ** -0.5, 0.03125)
    expert_ids_keys = jax.random.split(jax.random.fold_in(key_list[10], 1), TOKENS // TOK_DEV)
    expert_ids_turns = jax.random.permutation(jax.random.fold_in(key_list[10], 3), TOKENS // TOK_DEV)
    expert_ids = jax.vmap(lambda own, number: deal_out(jax.random.fold_in(key_list[10], 2), own, number, TOK_DEV, EXPERTS, TOPK, CAP, 2))(expert_ids_keys, expert_ids_turns).reshape((TOKENS, TOPK))
    gate_weight = scatter_about(key_list[11], (EXPERTS, D, FF), D ** -0.5, 0.125, ((0, 32), (2, 8)))
    up_weight = scatter_about(key_list[12], (EXPERTS, D, FF), D ** -0.5, 0.125, ((0, 32), (2, 8)))
    down_weight = scatter_about(key_list[13], (EXPERTS, FF, D), (32.0 * FF ** -0.5), 6.0, ((0, 32), (1, 8)))
    return {"tokens": tokens, "lengths": lengths, "page_table": page_table, "attention_gain": attention_gain, "query_weight": query_weight, "key_weight": key_weight, "value_weight": value_weight, "out_weight": out_weight, "expert_gain": expert_gain, "router_weight": router_weight, "expert_ids": expert_ids, "gate_weight": gate_weight, "up_weight": up_weight, "down_weight": down_weight}


epsilon = 1e-05
rope_base = 10000.0

def rms_scale(matrix, scaling):
    mean_square = lax.optimization_barrier(jnp.mean(matrix * matrix, axis=-1, keepdims=True))
    return matrix * lax.rsqrt(mean_square + epsilon) * scaling

def segment_info(lengths, places):
    starts = jnp.cumsum(lengths).astype(jnp.int32) - lengths
    inside = (places[:, None] >= starts[None, :]).astype(jnp.int32)
    segment = lax.optimization_barrier(jnp.sum(inside, axis=1)).astype(jnp.int32) - 1
    slot_ids = jnp.arange(starts.shape[0], dtype=jnp.int32)
    seg_start = lax.optimization_barrier(jnp.sum(jnp.where(slot_ids[None, :] == segment[:, None], starts[None, :], 0), axis=1)).astype(jnp.int32)
    return (segment, places - seg_start)

def rotate(matrix, position):
    half_dim = matrix.shape[-1] // 2
    frequency = jnp.exp(-jnp.log(rope_base) * jnp.arange(half_dim, dtype=jnp.float32) * (2.0 / matrix.shape[-1]))
    angles = position.astype(jnp.float32)[:, None] * frequency[None, :]
    cosine = jnp.cos(angles)[:, None, :]
    sine_part = jnp.sin(angles)[:, None, :]
    first_half = matrix[..., :half_dim]
    second = matrix[..., half_dim:]
    return jnp.concatenate([first_half * cosine - second * sine_part, second * cosine + first_half * sine_part], axis=-1)

def attend_block(query_part, query_places, query_segments, key_rows, value_rows, key_places, key_segments):
    scores = jnp.einsum('qhd,khd->hqk', query_part.astype(jnp.float32), key_rows.astype(jnp.float32)) * HEAD_DIM ** (-0.5)
    allowed = ((query_segments[:, None] == key_segments[None, :]) & (key_places[None, :] <= query_places[:, None]))[None]
    masked = jnp.where(allowed, scores, -1e+30)
    row_peak = lax.optimization_barrier(jnp.max(masked, axis=-1, keepdims=True))
    raised = jnp.where(allowed, jnp.exp(masked - row_peak), 0.0)
    row_total = lax.optimization_barrier(jnp.sum(raised, axis=-1))
    weights = lax.optimization_barrier(raised.astype(jnp.bfloat16)).astype(jnp.float32)
    weighted = jnp.einsum('hqk,khd->qhd', weights, value_rows.astype(jnp.float32))
    return (weighted / jnp.transpose(row_total)[:, :, None]).astype(jnp.bfloat16)

def reference(tokens, lengths, page_table, attention_gain, query_weight, key_weight, value_weight, out_weight, expert_gain, router_weight, expert_ids, gate_weight, up_weight, down_weight):
    places = jnp.arange(TOKENS, dtype=jnp.int32)
    segment, position = segment_info(lengths, places)
    stream = tokens.astype(jnp.float32)
    normed = rms_scale(stream, attention_gain).astype(jnp.bfloat16)
    queries = rotate(jnp.dot(normed, query_weight, preferred_element_type=jnp.float32).reshape(TOKENS, HEADS, HEAD_DIM), position).astype(jnp.bfloat16)
    key_rows = rotate(jnp.dot(normed, key_weight, preferred_element_type=jnp.float32).reshape(TOKENS, HEADS, HEAD_DIM), position).astype(jnp.bfloat16)
    value_rows = jnp.dot(normed, value_weight, preferred_element_type=jnp.float32).astype(jnp.bfloat16).reshape(TOKENS, HEADS, HEAD_DIM)
    block_rows = 512 if TOKENS % 512 == 0 else TOKENS
    block_count = TOKENS // block_rows

    def one_block(number):
        row_start = number * block_rows
        query_part = lax.dynamic_slice_in_dim(queries, row_start, block_rows, 0)
        query_places = lax.dynamic_slice_in_dim(places, row_start, block_rows, 0)
        query_segments = lax.dynamic_slice_in_dim(segment, row_start, block_rows, 0)
        return attend_block(query_part, query_places, query_segments, key_rows, value_rows, places, segment)
    attended = lax.map(one_block, jnp.arange(block_count, dtype=jnp.int32)).reshape(TOKENS, HEADS * HEAD_DIM)
    hidden = stream + jnp.dot(attended, out_weight, preferred_element_type=jnp.float32)
    moe_input = rms_scale(hidden, expert_gain).astype(jnp.bfloat16)
    probability = jax.nn.softmax(jnp.dot(moe_input, router_weight, preferred_element_type=jnp.float32), axis=-1)
    expert_range = jnp.arange(EXPERTS, dtype=jnp.int32)
    chosen = lax.optimization_barrier(jnp.sum(jnp.where(expert_ids[:, :, None] == expert_range[None, None, :], probability[:, None, :], 0.0), axis=-1))
    flat_ids = expert_ids.reshape(-1)
    onehot = (flat_ids[:, None] == expert_range[None, :]).astype(jnp.int32)
    slot_rank = lax.optimization_barrier(jnp.sum(jnp.cumsum(onehot, axis=0) * onehot, axis=1)).astype(jnp.int32) - 1
    room_size = N_SEQ * CAP
    owners = jnp.arange(TOKENS * TOPK, dtype=jnp.int32) // TOPK
    target = flat_ids * room_size + slot_rank
    row_table = jnp.full((EXPERTS * room_size,), TOKENS, jnp.int32).at[target].set(owners).reshape(EXPERTS, room_size)
    slot_scale = jnp.zeros((EXPERTS * room_size,), jnp.float32).at[target].set(chosen.reshape(-1)).reshape(EXPERTS, room_size)
    padded = jnp.concatenate([moe_input, jnp.zeros((1, D), jnp.bfloat16)], axis=0)

    def one_expert(running, operands):
        row_index, row_weight, gate_part, up_part, down_part = operands
        gathered = padded[row_index]
        gate_out = jnp.dot(gathered, gate_part, preferred_element_type=jnp.float32)
        up_out = jnp.dot(gathered, up_part, preferred_element_type=jnp.float32)
        activation = (jax.nn.silu(gate_out) * up_out).astype(jnp.bfloat16)
        pieces = jnp.einsum('rmf,mfd->mrd', activation.reshape(room_size, N_TENSOR, FF // N_TENSOR).astype(jnp.float32), down_part.reshape(N_TENSOR, FF // N_TENSOR, D).astype(jnp.float32))
        rounded = lax.optimization_barrier(pieces.astype(jnp.bfloat16)).astype(jnp.float32)
        result = lax.optimization_barrier(jnp.sum(rounded, axis=0)) * row_weight[:, None]
        return (running.at[row_index].add(result), None)
    mixture, _ = lax.scan(one_expert, jnp.zeros((TOKENS + 1, D), jnp.float32), (row_table, slot_scale, gate_weight, up_weight, down_weight))
    layer_out = (hidden + mixture[:TOKENS]).astype(jnp.bfloat16)
    span_size = HEADS * HEAD_DIM
    key_cache = jnp.zeros((PAGES, PAGE, span_size), jnp.bfloat16).at[page_table].set(key_rows.reshape(PAGES, PAGE, span_size))
    value_cache = jnp.zeros((PAGES, PAGE, span_size), jnp.bfloat16).at[page_table].set(value_rows.reshape(PAGES, PAGE, span_size))
    return (layer_out, key_cache, value_cache)
```

```python
import functools

import jax
import jax.numpy as jnp
from jax import lax
from jax.experimental import pallas as pl
from jax.experimental.pallas import tpu as pltpu
from jax.sharding import PartitionSpec as P

HEAD_DIM = 128
PAGE = 16
RING = 4
MESH = pl.DeviceIdType.MESH

epsilon = 1e-05
rope_base = 10000.0


def place():
    seq = lax.axis_index("seq")
    tensor = lax.axis_index("tensor")
    return seq // 8, (seq // 2) % RING, seq % 2, tensor // 2, tensor % 2


def device(z, x, core, y, low):
    z, x, y = (z + RING) % RING, (x + RING) % RING, (y + RING) % RING
    return ((z * RING + x) * 2 + core, y * 2 + low)


def greet(peers):
    barrier = pltpu.get_barrier_semaphore()
    for peer in peers:
        pl.semaphore_signal(barrier, inc=1, device_id=peer, device_id_type=MESH)
    pl.semaphore_wait(barrier, len(peers))


class Wires:
    def __init__(self, send_sems, recv_sems):
        self.send_sems, self.recv_sems, self.copies = send_sems, recv_sems, []

    def push(self, source, target, peer):
        number = len(self.copies)
        copy = pltpu.make_async_remote_copy(
            src_ref=source,
            dst_ref=target,
            send_sem=self.send_sems.at[number],
            recv_sem=self.recv_sems.at[number],
            device_id=peer,
            device_id_type=MESH,
        )
        copy.start()
        self.copies.append(copy)
        return copy

    def drain(self):
        for copy in self.copies:
            copy.wait_send()


def spread(wires, view, half, near, far, mate, a, b):
    def wrap(v):
        return (v + RING) % RING

    mates = []

    def share(a_at, b_at):
        piece = view(a_at, b_at)
        mates.append(wires.push(piece, piece, mate))

    def across(a_at):
        piece = view(a_at, b)
        ahead = wires.push(piece, piece, far(1))
        back = wires.push(piece, piece, far(-1))
        share(a_at, b)
        return ahead, back

    own = view(a, b)
    ahead = wires.push(own, own, near(1))
    back = wires.push(own, own, near(-1))
    origins = [a, wrap(a - 1), wrap(a + 1), wrap(a + 2)]
    pairs = [across(origins[0])]
    ahead.wait_recv()
    part = half(origins[1], b, 0)
    ahead = wires.push(part, part, near(1))
    pairs.append(across(origins[1]))
    back.wait_recv()
    part = half(origins[2], b, 1)
    back = wires.push(part, part, near(-1))
    pairs.append(across(origins[2]))
    ahead.wait_recv()
    back.wait_recv()
    pairs.append(across(origins[3]))
    relays = []
    for number, (ahead, back) in enumerate(pairs):
        ahead.wait_recv()
        if number < 2:
            piece = view(origins[number], wrap(b - 1))
            relays.append(wires.push(piece, piece, far(1)))
        share(origins[number], wrap(b - 1))
        back.wait_recv()
        if number >= 2:
            piece = view(origins[number], wrap(b + 1))
            relays.append(wires.push(piece, piece, far(-1)))
        share(origins[number], wrap(b + 1))
    for number, relay in enumerate(relays):
        relay.wait_recv()
        share(origins[number], wrap(b + 2))
    for copy in mates:
        copy.wait_recv()


def gather_stream_kernel(mine, out, send_sems, recv_sems, local_sem):
    z, x, core, y, low = place()
    near = lambda step: device(z + step, x, core, y, low)
    far = lambda step: device(z, x + step, core, y, low)
    mate = device(z, x, 1 - core, y, low)
    greet([near(1), near(-1), far(1), far(-1), mate])
    local = pltpu.make_async_copy(mine, out.at[z, x, core], local_sem)
    local.start()
    local.wait()
    rows = mine.shape[0] // 2
    wires = Wires(send_sems, recv_sems)
    spread(
        wires,
        lambda a, b: out.at[a, b, core],
        lambda a, b, part: out.at[a, b, core, pl.ds(part * rows, rows)],
        near,
        far,
        mate,
        z,
        x,
    )
    wires.drain()


def gather_stream(mine):
    rows, columns = mine.shape
    copies = 4 + 8 + 4 + 16
    return pl.pallas_call(
        gather_stream_kernel,
        out_shape=jax.ShapeDtypeStruct((RING, RING, 2, rows, columns), mine.dtype),
        in_specs=[pl.BlockSpec(memory_space=pltpu.VMEM)],
        out_specs=pl.BlockSpec(memory_space=pl.ANY),
        scratch_shapes=[
            pltpu.SemaphoreType.DMA((copies,)),
            pltpu.SemaphoreType.DMA((copies,)),
            pltpu.SemaphoreType.DMA,
        ],
        compiler_params=pltpu.CompilerParams(collective_id=0, has_side_effects=True),
        name="gather_stream",
    )(mine).reshape(RING * RING * 2 * rows, columns)


def gather_all_kernel(mine, out, send_sems, recv_sems, local_sem):
    z, x, core, y, low = place()
    up = lambda step: device(z + step, x, core, y, low)
    twin = device(z, x, core, y, 1 - low)
    near = lambda step: device(z, x + step * (1 - core), core, y + step * core, low)
    far = lambda step: device(z, x + step * core, core, y + step * (1 - core), low)
    mate = device(z, x, 1 - core, y, low)
    greet([up(1), up(-1), twin, near(1), near(-1), far(1), far(-1), mate])
    wires = Wires(send_sems, recv_sems)
    local = pltpu.make_async_copy(mine, out.at[z, x, core, y, low], local_sem)
    local.start()
    copy = wires.push(mine, out.at[z, x, core, y, low], twin)
    local.wait()
    copy.wait_recv()
    both = out.at[z, x, core, y]
    ahead = wires.push(both, both, up(1))
    back = wires.push(both, both, up(-1))
    ahead.wait_recv()
    part = out.at[(z + 3) % RING, x, core, y, 0]
    ahead = wires.push(part, part, up(1))
    back.wait_recv()
    part = out.at[(z + 1) % RING, x, core, y, 1]
    back = wires.push(part, part, up(-1))
    ahead.wait_recv()
    back.wait_recv()

    def view(a, b):
        return out.at[:, a * (1 - core) + b * core, core, b * (1 - core) + a * core]

    def half(a, b, part):
        return out.at[
            pl.ds(part * 2, 2), a * (1 - core) + b * core, core, b * (1 - core) + a * core
        ]

    spread(
        wires, view, half, near, far, mate, x * (1 - core) + y * core, y * (1 - core) + x * core
    )
    wires.drain()


def gather_all(mine):
    rows, columns = mine.shape
    copies = 1 + 4 + 4 + 8 + 4 + 16
    return pl.pallas_call(
        gather_all_kernel,
        out_shape=jax.ShapeDtypeStruct((RING, RING, 2, RING, 2, rows, columns), mine.dtype),
        in_specs=[pl.BlockSpec(memory_space=pltpu.VMEM)],
        out_specs=pl.BlockSpec(memory_space=pl.ANY),
        scratch_shapes=[
            pltpu.SemaphoreType.DMA((copies,)),
            pltpu.SemaphoreType.DMA((copies,)),
            pltpu.SemaphoreType.DMA,
        ],
        compiler_params=pltpu.CompilerParams(collective_id=1, has_side_effects=True),
        name="gather_all",
    )(mine).reshape(RING * RING * 2 * RING * 2 * rows, columns)


def tensor_peers():
    seq, tensor = lax.axis_index("seq"), lax.axis_index("tensor")
    return [(seq, (tensor + step) % 8) for step in range(1, 8)]


def scatter_tensor_kernel(parts, out, landed, send_sems, recv_sems):
    tensor = lax.axis_index("tensor")
    peers = tensor_peers()
    greet(peers)
    wires = Wires(send_sems, recv_sems)
    for number, peer in enumerate(peers):
        wires.push(parts.at[peer[1]], landed.at[number], peer)
    total = parts[tensor].astype(jnp.float32)
    for number, copy in enumerate(wires.copies):
        copy.wait_recv()
        total = total + landed[number].astype(jnp.float32)
    out[...] = total
    wires.drain()


def scatter_tensor(parts):
    rows, columns = parts.shape[0] // 8, parts.shape[1]
    return pl.pallas_call(
        scatter_tensor_kernel,
        out_shape=jax.ShapeDtypeStruct((rows, columns), jnp.float32),
        in_specs=[pl.BlockSpec(memory_space=pltpu.VMEM)],
        out_specs=pl.BlockSpec(memory_space=pltpu.VMEM),
        scratch_shapes=[
            pltpu.VMEM((7, rows, columns), parts.dtype),
            pltpu.SemaphoreType.DMA((7,)),
            pltpu.SemaphoreType.DMA((7,)),
        ],
        compiler_params=pltpu.CompilerParams(collective_id=2, has_side_effects=True),
        name="scatter_tensor",
    )(parts.reshape(8, rows, columns))


def gather_tensor_kernel(mine, out, send_sems, recv_sems, local_sem):
    tensor = lax.axis_index("tensor")
    peers = tensor_peers()
    greet(peers)
    wires = Wires(send_sems, recv_sems)
    for peer in peers:
        wires.push(mine, out.at[tensor], peer)
    local = pltpu.make_async_copy(mine, out.at[tensor], local_sem)
    local.start()
    local.wait()
    for copy in wires.copies:
        copy.wait_recv()
    wires.drain()


def gather_tensor(mine):
    rows, columns = mine.shape
    return pl.pallas_call(
        gather_tensor_kernel,
        out_shape=jax.ShapeDtypeStruct((8, rows, columns), mine.dtype),
        in_specs=[pl.BlockSpec(memory_space=pltpu.VMEM)],
        out_specs=pl.BlockSpec(memory_space=pl.ANY),
        scratch_shapes=[
            pltpu.SemaphoreType.DMA((7,)),
            pltpu.SemaphoreType.DMA((7,)),
            pltpu.SemaphoreType.DMA,
        ],
        compiler_params=pltpu.CompilerParams(collective_id=3, has_side_effects=True),
        name="gather_tensor",
    )(mine).reshape(8 * rows, columns)


def scatter_all_kernel(
    parts, out, held, pair, far_relay, far_land, near_relay, near_land, up_relay, up_land, twin_land,
    send_sems, recv_sems, local_sems,
):
    z, x, core, y, low = place()
    up = lambda step: device(z + step, x, core, y, low)
    twin = device(z, x, core, y, 1 - low)
    near = lambda step: device(z, x + step * (1 - core), core, y + step * core, low)
    far = lambda step: device(z, x + step * core, core, y + step * (1 - core), low)
    mate = device(z, x, 1 - core, y, low)
    greet([up(1), up(-1), twin, near(1), near(-1), far(1), far(-1), mate])
    wires = Wires(send_sems, recv_sems)
    shifts = (2, 1, 3, 0)

    def piece(side, i, j):
        a = (x * (1 - side) + y * side + shifts[i]) % RING
        b = (y * (1 - side) + x * side + shifts[j]) % RING
        return parts.at[:, a * (1 - side) + b * side, side, b * (1 - side) + a * side]

    order = [(0, 0), (1, 0), (0, 1), (0, 2), (2, 0), (1, 1), (1, 2), (3, 0)]
    order += [(2, 1), (2, 2), (0, 3), (3, 1), (3, 2), (1, 3), (2, 3), (3, 3)]
    pairs, locals_ = {}, {}
    for i, j in order:
        k = i * RING + j
        pairs[k] = wires.push(piece(1 - core, i, j), pair.at[k], mate)
        locals_[k] = pltpu.make_async_copy(piece(core, i, j), held.at[k], local_sems.at[k])
        locals_[k].start()

    def add(target, first, count, sources):
        @pl.loop(0, count)
        def _(n):
            total = target[first + n].astype(jnp.float32)
            for source in sources:
                total = total + source[n].astype(jnp.float32)
            target[first + n] = total.astype(jnp.bfloat16)

    def meet(k):
        pairs[k].wait_recv()
        locals_[k].wait()

    relays, lands = {}, {}

    def opening(i):
        k = i * RING
        meet(k)
        add(held.at[k], 0, 4, [pair.at[k]])
        relays[i] = (
            wires.push(held.at[k, pl.ds(0, 2)], far_relay.at[i, 0], far(1)),
            wires.push(held.at[k, pl.ds(2, 2)], far_relay.at[i, 1], far(-1)),
        )

    def middle(i):
        for side, step in ((0, 1), (1, -1)):
            k = i * RING + 1 + side
            meet(k)
            add(held.at[k], 2 - 2 * side, 2, [pair.at[k, pl.ds(2 - 2 * side, 2)]])
            relays[i][side].wait_recv()
            add(held.at[k], 2 * side, 2, [pair.at[k, pl.ds(2 * side, 2)], far_relay.at[i, side]])
            lands[i, side] = wires.push(held.at[k], far_land.at[i, side], far(step))

    def closing(i):
        k = i * RING + 3
        meet(k)
        lands[i, 0].wait_recv()
        lands[i, 1].wait_recv()
        add(held.at[k], 0, 4, [pair.at[k], far_land.at[i, 0], far_land.at[i, 1]])

    opening(0)
    opening(1)
    middle(0)
    opening(2)
    middle(1)
    opening(3)
    middle(2)
    closing(0)
    near_copies = (
        wires.push(held.at[3, pl.ds(0, 2)], near_relay.at[0], near(1)),
        wires.push(held.at[3, pl.ds(2, 2)], near_relay.at[1], near(-1)),
    )
    middle(3)
    near_lands = []
    for side, step in ((0, 1), (1, -1)):
        closing(1 + side)
        near_copies[side].wait_recv()
        k = (1 + side) * RING + 3
        add(held.at[k], 2 * side, 2, [near_relay.at[side]])
        near_lands.append(wires.push(held.at[k], near_land.at[side], near(step)))
    closing(3)
    for copy in near_lands:
        copy.wait_recv()
    last = held.at[15]
    add(last, 0, 4, [near_land.at[0], near_land.at[1]])
    rows = out.shape[0]
    beyond = (z + 2) % RING
    up_copies = [
        wires.push(last.at[beyond, pl.ds(side * rows, rows)], up_relay.at[side], up(step))
        for side, step in ((0, 1), (1, -1))
    ]
    up_lands = []
    for side, step in ((0, 1), (1, -1)):
        up_copies[side].wait_recv()
        beside = (z + step + RING) % RING
        span = pl.ds(side * rows, rows)
        total = last[beside, span].astype(jnp.float32) + up_relay[side].astype(jnp.float32)
        last[beside, span] = total.astype(jnp.bfloat16)
        up_lands.append(wires.push(last.at[beside], up_land.at[side], up(step)))
    for copy in up_lands:
        copy.wait_recv()
    total = last[z].astype(jnp.float32)
    total = total + up_land[0].astype(jnp.float32) + up_land[1].astype(jnp.float32)
    last[z] = total.astype(jnp.bfloat16)
    other = pl.multiple_of((1 - low) * rows, rows)
    mine = pl.multiple_of(low * rows, rows)
    copy = wires.push(last.at[z, pl.ds(other, rows)], twin_land, twin)
    copy.wait_recv()
    out[...] = last[z, pl.ds(mine, rows)].astype(jnp.float32) + twin_land[...].astype(jnp.float32)
    wires.drain()


def scatter_all(parts):
    rows, columns = parts.shape[0] // (RING * RING * 2 * RING * 2), parts.shape[1]
    two = 2 * rows
    copies = 16 + 16 + 4 + 4 + 1
    grain = (RING, two, columns)
    halves = (2, two, columns)
    scratch = lambda *shape: pltpu.VMEM(shape, parts.dtype)
    return pl.pallas_call(
        scatter_all_kernel,
        out_shape=jax.ShapeDtypeStruct((rows, columns), jnp.float32),
        in_specs=[pl.BlockSpec(memory_space=pl.ANY)],
        out_specs=pl.BlockSpec(memory_space=pltpu.VMEM),
        scratch_shapes=[
            scratch(16, *grain),
            scratch(16, *grain),
            scratch(RING, 2, *halves),
            scratch(RING, 2, *grain),
            scratch(2, *halves),
            scratch(2, *grain),
            scratch(2, rows, columns),
            scratch(2, two, columns),
            scratch(rows, columns),
            pltpu.SemaphoreType.DMA((copies,)),
            pltpu.SemaphoreType.DMA((copies,)),
            pltpu.SemaphoreType.DMA((16,)),
        ],
        compiler_params=pltpu.CompilerParams(
            collective_id=4, has_side_effects=True, vmem_limit_bytes=40 * 1024 * 1024
        ),
        name="scatter_all",
    )(parts.reshape(RING, RING, 2, RING, two, columns))


def pages_kernel(blocks, kv, keys, values):
    columns = keys.shape[-1]
    keys[...] = kv[:, :, :columns]
    values[...] = kv[:, :, columns:]


def write_pages(kv, blocks, columns):
    count = blocks.shape[0]
    out = jax.ShapeDtypeStruct((count, PAGE, columns), kv.dtype)
    spec = pl.BlockSpec((1, PAGE, columns), lambda j, blocks: (j, 0, 0))
    return pl.pallas_call(
        pages_kernel,
        out_shape=(out, out),
        grid_spec=pltpu.PrefetchScalarGridSpec(
            num_scalar_prefetch=1,
            grid=(count,),
            in_specs=[pl.BlockSpec((1, PAGE, 2 * columns), lambda j, blocks: (blocks[j], 0, 0))],
            out_specs=(spec, spec),
        ),
        name="write_pages",
    )(blocks, kv.reshape(-1, PAGE, 2 * columns))


def rms_scale(matrix, scaling):
    mean_square = jnp.mean(matrix * matrix, axis=-1, keepdims=True)
    return matrix * lax.rsqrt(mean_square + epsilon) * scaling


def segment_info(lengths, places):
    starts = jnp.cumsum(lengths) - lengths
    inside = (places[:, None] >= starts[None, :]).astype(jnp.int32)
    segment = jnp.sum(inside, axis=1) - 1
    slot_ids = jnp.arange(starts.shape[0], dtype=jnp.int32)
    seg_start = jnp.sum(
        jnp.where(slot_ids[None, :] == segment[:, None], starts[None, :], 0), axis=1
    )
    return (segment, places - seg_start)


def rotate(matrix, position):
    half_dim = matrix.shape[-1] // 2
    frequency = jnp.exp(
        -jnp.log(rope_base) * jnp.arange(half_dim, dtype=jnp.float32) * (2.0 / matrix.shape[-1])
    )
    angles = position.astype(jnp.float32)[:, None] * frequency[None, :]
    cosine = jnp.cos(angles)[:, None, :]
    sine_part = jnp.sin(angles)[:, None, :]
    first_half = matrix[..., :half_dim]
    second = matrix[..., half_dim:]
    return jnp.concatenate(
        [first_half * cosine - second * sine_part, second * cosine + first_half * sine_part],
        axis=-1,
    )


def local(
    tokens,
    lengths,
    page_table,
    attention_gain,
    query_weight,
    key_weight,
    value_weight,
    out_weight,
    expert_gain,
    router_weight,
    expert_ids,
    gate_weight,
    up_weight,
    down_weight,
):
    row_count = tokens.shape[0]
    feature_count = tokens.shape[1]
    span_size = query_weight.shape[1]
    head_count = span_size // HEAD_DIM
    shard_id = lax.axis_index("seq")
    places = shard_id * row_count + jnp.arange(row_count, dtype=jnp.int32)
    segment, position = segment_info(lengths, places)
    stream = tokens.astype(jnp.float32)
    normed = rms_scale(stream, attention_gain).astype(jnp.bfloat16)

    def project(weight):
        return jnp.dot(normed, weight, preferred_element_type=jnp.float32)

    def turned(matrix):
        return rotate(matrix.reshape(row_count, head_count, HEAD_DIM), position).astype(
            jnp.bfloat16
        )

    key_rows = turned(project(key_weight)).reshape(row_count, span_size)
    value_rows = project(value_weight).astype(jnp.bfloat16)
    kv = gather_stream(jnp.concatenate([key_rows, value_rows], axis=1))
    queries = turned(project(query_weight))

    page_rows = row_count // PAGE
    my_pages = shard_id * page_rows + jnp.arange(page_rows, dtype=jnp.int32)
    block_ids = jnp.arange(page_table.shape[0], dtype=jnp.int32)
    blocks = jnp.sum(
        jnp.where(page_table[None, :] == my_pages[:, None], block_ids[None, :], 0), axis=1
    )
    key_cache, value_cache = write_pages(kv, blocks, span_size)

    piece_rows = kv.shape[0]
    key_places = jnp.arange(piece_rows, dtype=jnp.int32)
    key_segments, _ = segment_info(lengths, key_places)
    scores = jnp.einsum(
        "qhd,khd->hqk",
        queries,
        kv[:, :span_size].reshape(piece_rows, head_count, HEAD_DIM),
        preferred_element_type=jnp.float32,
    ) * (HEAD_DIM ** (-0.5))
    allowed = (
        (segment[:, None] == key_segments[None, :]) & (key_places[None, :] <= places[:, None])
    )[None]
    peak = jnp.max(jnp.where(allowed, scores, -1e30), axis=-1)
    raised = jnp.where(allowed, jnp.exp(scores - peak[:, :, None]), 0.0)
    row_total = jnp.sum(raised, axis=-1)
    weighted = jnp.einsum(
        "hqk,khd->hqd",
        raised.astype(jnp.bfloat16),
        kv[:, span_size:].reshape(piece_rows, head_count, HEAD_DIM),
        preferred_element_type=jnp.float32,
    )
    attended = (
        jnp.transpose(weighted / row_total[:, :, None], (1, 0, 2))
        .reshape(row_count, span_size)
        .astype(jnp.bfloat16)
    )
    head_part = jnp.dot(attended, out_weight, preferred_element_type=jnp.float32)

    member = lax.axis_index("tensor")
    own_rows = row_count // lax.axis_size("tensor")
    own_stream = lax.dynamic_slice_in_dim(tokens, member * own_rows, own_rows, 0)
    own_ids = lax.dynamic_slice_in_dim(expert_ids, member * own_rows, own_rows, 0)
    hidden = own_stream.astype(jnp.float32) + scatter_tensor(head_part.astype(jnp.bfloat16))
    moe_input = rms_scale(hidden, expert_gain).astype(jnp.bfloat16)
    expert_count = router_weight.shape[1]
    probability = jax.nn.softmax(
        jnp.dot(moe_input, router_weight, preferred_element_type=jnp.float32), axis=-1
    )
    expert_range = jnp.arange(expert_count, dtype=jnp.int32)
    named = jnp.any(own_ids[:, :, None] == expert_range[None, None, :], axis=1)
    share = jnp.where(named, probability, 0.0)
    share_high = share.astype(jnp.bfloat16)
    share_low = (share - share_high.astype(jnp.float32)).astype(jnp.bfloat16)

    everyone = gather_all(jnp.concatenate([moe_input, share_high, share_low], axis=1))
    rows = everyone[:, :feature_count]
    local_count = gate_weight.shape[0]
    part = None
    for number in range(local_count):
        expert = shard_id * local_count + number
        mine = (jnp.arange(2 * expert_count, dtype=jnp.int32) % expert_count == expert)[None, :]
        scale = jnp.sum(
            jnp.where(mine, everyone[:, feature_count:].astype(jnp.float32), 0.0),
            axis=1,
            keepdims=True,
        )
        gate_out = jnp.dot(rows, gate_weight[number], preferred_element_type=jnp.float32)
        up_out = jnp.dot(rows, up_weight[number], preferred_element_type=jnp.float32)
        activation = (jax.nn.silu(gate_out) * up_out * scale).astype(jnp.bfloat16)
        term = jnp.dot(activation, down_weight[number], preferred_element_type=jnp.float32)
        part = term if part is None else part + term
    mixture = scatter_all(part.astype(jnp.bfloat16))
    layer_out = gather_tensor((hidden + mixture).astype(jnp.bfloat16))
    return (layer_out, key_cache, value_cache)


def solution(mesh):
    return jax.shard_map(
        local,
        mesh=mesh,
        in_specs=(
            P("seq", None),
            P(),
            P(),
            P(),
            P(None, "tensor"),
            P(None, "tensor"),
            P(None, "tensor"),
            P("tensor", None),
            P(),
            P(),
            P("seq", None),
            P("seq", None, "tensor"),
            P("seq", None, "tensor"),
            P("seq", "tensor", None),
        ),
        out_specs=(P("seq", None), P("seq", None, "tensor"), P("seq", None, "tensor")),
        check_vma=False,
    )
```

```python
import functools

import jax
import jax.numpy as jnp
from jax import lax
from jax.experimental import pallas as pl
from jax.experimental.pallas import tpu as pltpu
from jax.sharding import PartitionSpec as P

HEAD_DIM = 128
PAGE = 16
RING = 4
MESH = pl.DeviceIdType.MESH

epsilon = 1e-05
rope_base = 10000.0


def place():
    seq = lax.axis_index("seq")
    tensor = lax.axis_index("tensor")
    return seq // 8, (seq // 2) % RING, seq % 2, tensor // 2, tensor % 2


def device(z, x, core, y, low):
    z, x, y = (z + RING) % RING, (x + RING) % RING, (y + RING) % RING
    return ((z * RING + x) * 2 + core, y * 2 + low)


def greet(peers):
    barrier = pltpu.get_barrier_semaphore()
    for peer in peers:
        pl.semaphore_signal(barrier, inc=1, device_id=peer, device_id_type=MESH)
    pl.semaphore_wait(barrier, len(peers))


class Wires:
    def __init__(self, send_sems, recv_sems):
        self.send_sems, self.recv_sems, self.copies = send_sems, recv_sems, []

    def push(self, source, target, peer):
        number = len(self.copies)
        copy = pltpu.make_async_remote_copy(
            src_ref=source,
            dst_ref=target,
            send_sem=self.send_sems.at[number],
            recv_sem=self.recv_sems.at[number],
            device_id=peer,
            device_id_type=MESH,
        )
        copy.start()
        self.copies.append(copy)
        return copy

    def drain(self):
        for copy in self.copies:
            copy.wait_send()


def spread(wires, view, half, near, far, mate, a, b):
    def wrap(v):
        return (v + RING) % RING

    mates = []

    def share(a_at, b_at):
        piece = view(a_at, b_at)
        mates.append(wires.push(piece, piece, mate))

    def across(a_at):
        piece = view(a_at, b)
        ahead = wires.push(piece, piece, far(1))
        back = wires.push(piece, piece, far(-1))
        share(a_at, b)
        return ahead, back

    own = view(a, b)
    ahead = wires.push(own, own, near(1))
    back = wires.push(own, own, near(-1))
    origins = [a, wrap(a - 1), wrap(a + 1), wrap(a + 2)]
    pairs = [across(origins[0])]
    ahead.wait_recv()
    part = half(origins[1], b, 0)
    ahead = wires.push(part, part, near(1))
    pairs.append(across(origins[1]))
    back.wait_recv()
    part = half(origins[2], b, 1)
    back = wires.push(part, part, near(-1))
    pairs.append(across(origins[2]))
    ahead.wait_recv()
    back.wait_recv()
    pairs.append(across(origins[3]))
    relays = []
    for number, (ahead, back) in enumerate(pairs):
        ahead.wait_recv()
        if number < 2:
            piece = view(origins[number], wrap(b - 1))
            relays.append(wires.push(piece, piece, far(1)))
        share(origins[number], wrap(b - 1))
        back.wait_recv()
        if number >= 2:
            piece = view(origins[number], wrap(b + 1))
            relays.append(wires.push(piece, piece, far(-1)))
        share(origins[number], wrap(b + 1))
    for number, relay in enumerate(relays):
        relay.wait_recv()
        share(origins[number], wrap(b + 2))
    for copy in mates:
        copy.wait_recv()


def gather_stream_kernel(mine, out, send_sems, recv_sems, local_sem):
    z, x, core, y, low = place()
    near = lambda step: device(z + step, x, core, y, low)
    far = lambda step: device(z, x + step, core, y, low)
    mate = device(z, x, 1 - core, y, low)
    greet([near(1), near(-1), far(1), far(-1), mate])
    local = pltpu.make_async_copy(mine, out.at[z, x, core], local_sem)
    local.start()
    local.wait()
    rows = mine.shape[0] // 2
    wires = Wires(send_sems, recv_sems)
    spread(
        wires,
        lambda a, b: out.at[a, b, core],
        lambda a, b, part: out.at[a, b, core, pl.ds(part * rows, rows)],
        near,
        far,
        mate,
        z,
        x,
    )
    wires.drain()


def gather_stream(mine):
    rows, columns = mine.shape
    copies = 4 + 8 + 4 + 16
    return pl.pallas_call(
        gather_stream_kernel,
        out_shape=jax.ShapeDtypeStruct((RING, RING, 2, rows, columns), mine.dtype),
        in_specs=[pl.BlockSpec(memory_space=pltpu.VMEM)],
        out_specs=pl.BlockSpec(memory_space=pl.ANY),
        scratch_shapes=[
            pltpu.SemaphoreType.DMA((copies,)),
            pltpu.SemaphoreType.DMA((copies,)),
            pltpu.SemaphoreType.DMA,
        ],
        compiler_params=pltpu.CompilerParams(collective_id=0, has_side_effects=True),
        name="gather_stream",
    )(mine).reshape(RING * RING * 2 * rows, columns)


def tensor_peers():
    seq, tensor = lax.axis_index("seq"), lax.axis_index("tensor")
    return [(seq, (tensor + step) % 8) for step in range(1, 8)]


def scatter_tensor_kernel(parts, out, landed, send_sems, recv_sems):
    tensor = lax.axis_index("tensor")
    peers = tensor_peers()
    greet(peers)
    wires = Wires(send_sems, recv_sems)
    for number, peer in enumerate(peers):
        wires.push(parts.at[peer[1]], landed.at[number], peer)
    total = parts[tensor].astype(jnp.float32)
    for number, copy in enumerate(wires.copies):
        copy.wait_recv()
        total = total + landed[number].astype(jnp.float32)
    out[...] = total
    wires.drain()


def scatter_tensor(parts):
    rows, columns = parts.shape[0] // 8, parts.shape[1]
    return pl.pallas_call(
        scatter_tensor_kernel,
        out_shape=jax.ShapeDtypeStruct((rows, columns), jnp.float32),
        in_specs=[pl.BlockSpec(memory_space=pltpu.VMEM)],
        out_specs=pl.BlockSpec(memory_space=pltpu.VMEM),
        scratch_shapes=[
            pltpu.VMEM((7, rows, columns), parts.dtype),
            pltpu.SemaphoreType.DMA((7,)),
            pltpu.SemaphoreType.DMA((7,)),
        ],
        compiler_params=pltpu.CompilerParams(collective_id=2, has_side_effects=True),
        name="scatter_tensor",
    )(parts.reshape(8, rows, columns))


def mixture_kernel(
    mine, hidden, gate, up_part, down, out, rows_all, held, outbox, pair, near_relay, near_land,
    far_relay, far_land, up_relay, up_land, twin_land, final, weight_in, weight_out,
    send_sems, recv_sems, local_sems,
):
    z, x, core, y, low = place()
    up = lambda step: device(z + step, x, core, y, low)
    twin = device(z, x, core, y, 1 - low)
    near = lambda step: device(z, x + step * (1 - core), core, y + step * core, low)
    far = lambda step: device(z, x + step * core, core, y + step * (1 - core), low)
    mate = device(z, x, 1 - core, y, low)
    a, b = x * (1 - core) + y * core, y * (1 - core) + x * core
    peers = tensor_peers()
    ring_y = [near(1), near(-1), far(1), far(-1)]
    greet([up(1), up(-1), mate] + ring_y + peers)
    wires = Wires(send_sems, recv_sems)
    features, width = down.shape[2], gate.shape[2]
    experts_here = gate.shape[0]
    rows = mine.shape[0]

    span = lambda member: pl.ds(pl.multiple_of(member * rows, rows), rows)
    place_own = rows_all.at[z, x, core, y, span(low)]
    loads = [pltpu.make_async_copy(mine, place_own, local_sems.at[0])]
    for number in range(experts_here):
        for kind, source in enumerate((gate, up_part)):
            column = (kind * experts_here + number) * width
            loads.append(
                pltpu.make_async_copy(
                    source.at[number],
                    weight_in.at[:, pl.ds(column, width)],
                    local_sems.at[len(loads)],
                )
            )
        loads.append(
            pltpu.make_async_copy(
                down.at[number],
                weight_out.at[pl.ds(number * width, width)],
                local_sems.at[len(loads)],
            )
        )
    for load in loads:
        load.start()

    def wrap(v):
        return (v + RING) % RING

    def view(side, a_at, b_at, first=0, count=RING):
        return rows_all.at[
            pl.ds(first, count),
            a_at * (1 - side) + b_at * side,
            side,
            b_at * (1 - side) + a_at * side,
        ]

    copy = wires.push(mine, place_own, twin)
    loads[0].wait()
    copy.wait_recv()
    both = rows_all.at[z, x, core, y]
    ahead = wires.push(both, both, up(1))
    back = wires.push(both, both, up(-1))
    ahead.wait_recv()
    piece = rows_all.at[wrap(z - 1), x, core, y, pl.ds(0, rows)]
    ahead = wires.push(piece, piece, up(1))
    back.wait_recv()
    piece = rows_all.at[wrap(z + 1), x, core, y, pl.ds(rows, rows)]
    back = wires.push(piece, piece, up(-1))
    ahead.wait_recv()
    back.wait_recv()

    mates = []

    def share(a_at, b_at):
        piece = view(core, a_at, b_at)
        mates.append(wires.push(piece, piece, mate))

    def across(a_at):
        piece = view(core, a_at, b)
        ahead = wires.push(piece, piece, far(1))
        back = wires.push(piece, piece, far(-1))
        share(a_at, b)
        return ahead, back

    own = view(core, a, b)
    ahead = wires.push(own, own, near(1))
    back = wires.push(own, own, near(-1))
    origins = [a, wrap(a - 1), wrap(a + 1), wrap(a + 2)]
    pairs = [across(origins[0])]
    ahead.wait_recv()
    piece = view(core, origins[1], b, 0, 2)
    ahead = wires.push(piece, piece, near(1))
    pairs.append(across(origins[1]))
    back.wait_recv()
    piece = view(core, origins[2], b, 2, 2)
    back = wires.push(piece, piece, near(-1))
    pairs.append(across(origins[2]))
    ahead.wait_recv()
    back.wait_recv()
    pairs.append(across(origins[3]))

    relays = []

    def onward(number):
        ahead, back = pairs[number]
        ahead.wait_recv()
        if number < 2:
            piece = view(core, origins[number], wrap(b - 1))
            relays.append(wires.push(piece, piece, far(1)))
        share(origins[number], wrap(b - 1))
        back.wait_recv()
        if number >= 2:
            piece = view(core, origins[number], wrap(b + 1))
            relays.append(wires.push(piece, piece, far(-1)))
        share(origins[number], wrap(b + 1))

    lines = (0, 3, 1, 2)
    first_expert = lax.axis_index("seq") * experts_here
    inner = experts_here * width

    def experts(side, line, target):
        a_side, b_side = x * (1 - side) + y * side, y * (1 - side) + x * side
        b_at = (b_side + lines[line]) % RING

        @pl.loop(0, RING)
        def _(i):
            a_at = (a_side + 2 + 3 * i) % RING
            block = rows_all[
                :, a_at * (1 - side) + b_at * side, side, b_at * (1 - side) + a_at * side
            ]
            block = block.reshape(RING * 2 * rows, block.shape[-1])
            product = jnp.dot(
                block[:, :features], weight_in[...], preferred_element_type=jnp.float32
            )
            shares = block[:, features:].astype(jnp.float32)
            names = lax.broadcasted_iota(jnp.int32, shares.shape, 1) % (shares.shape[1] // 2)
            scales = [
                jnp.broadcast_to(
                    jnp.sum(
                        jnp.where(names == first_expert + number, shares, 0.0),
                        axis=1,
                        keepdims=True,
                    ),
                    (shares.shape[0], width),
                )
                for number in range(experts_here)
            ]
            gated = product[:, :inner]
            active = gated / (1.0 + jnp.exp(-gated)) * product[:, inner:]
            active = (active * jnp.concatenate(scales, axis=1)).astype(jnp.bfloat16)
            term = jnp.dot(active, weight_out[...], preferred_element_type=jnp.float32)
            target[line * RING + i] = term.astype(jnp.bfloat16).reshape(RING, 2 * rows, features)

    exchanges = {}

    def swap(line):
        for i in (0, 1, 3, 2):
            k = line * RING + i
            exchanges[k] = wires.push(outbox.at[k], pair.at[k], mate)

    def ours(line):
        experts(core, line, held)

    def theirs(line, numbers):
        for number in numbers:
            mates[number].wait_recv()
        experts(1 - core, line, outbox)
        swap(line)

    def add(target, first, count, sources):
        @pl.loop(0, count)
        def _(n):
            total = target[first + n].astype(jnp.float32)
            for source in sources:
                total = total + source[n].astype(jnp.float32)
            target[first + n] = total.astype(jnp.bfloat16)

    turns = {}
    lands = {}

    def opening(line):
        k = line * RING
        exchanges[k].wait_recv()
        add(held.at[k], 0, RING, [pair.at[k]])
        turns[line] = (
            wires.push(held.at[k, pl.ds(0, 2)], near_relay.at[line, 0], near(1)),
            wires.push(held.at[k, pl.ds(2, 2)], near_relay.at[line, 1], near(-1)),
        )

    def middle(line):
        for side, i, step in ((0, 1, 1), (1, 3, -1)):
            k = line * RING + i
            exchanges[k].wait_recv()
            add(held.at[k], 2 - 2 * side, 2, [pair.at[k, pl.ds(2 - 2 * side, 2)]])
            turns[line][side].wait_recv()
            add(held.at[k], 2 * side, 2, [pair.at[k, pl.ds(2 * side, 2)], near_relay.at[line, side]])
            lands[line, side] = wires.push(held.at[k], near_land.at[line, side], near(step))

    def closing(line):
        k = line * RING + 2
        exchanges[k].wait_recv()
        lands[line, 0].wait_recv()
        lands[line, 1].wait_recv()
        add(held.at[k], 0, RING, [pair.at[k], near_land.at[line, 0], near_land.at[line, 1]])

    def relayed(number):
        relays[number].wait_recv()
        share(origins[number], wrap(b + 2))

    onward(0)
    for load in loads[1:]:
        load.wait()
    ours(0)
    onward(1)
    theirs(0, (0, 1, 2, 3))
    onward(2)
    opening(0)
    onward(3)
    ours(1)
    middle(0)
    relayed(0)
    relayed(1)
    theirs(1, (4, 6, 8, 10))
    opening(1)
    closing(0)
    ours(2)
    relayed(2)
    relayed(3)
    middle(1)
    theirs(2, (5, 7, 9, 11))
    opening(2)
    closing(1)
    ours(3)
    middle(2)
    theirs(3, (12, 13, 14, 15))
    opening(3)
    closing(2)
    middle(3)
    closing(3)

    line_sum = lambda line: held.at[line * RING + 2]
    far_turns = (
        wires.push(held.at[3 * RING + 2, pl.ds(0, 2)], far_relay.at[0], far(1)),
        wires.push(held.at[3 * RING + 2, pl.ds(2, 2)], far_relay.at[1], far(-1)),
    )
    far_lands = []
    for side, line, step in ((0, 2, 1), (1, 1, -1)):
        far_turns[side].wait_recv()
        add(line_sum(line), 2 * side, 2, [far_relay.at[side]])
        far_lands.append(wires.push(line_sum(line), far_land.at[side], far(step)))
    for copy in far_lands:
        copy.wait_recv()
    last = line_sum(0)
    add(last, 0, RING, [far_land.at[0], far_land.at[1]])

    beyond = wrap(z + 2)
    up_turns = [
        wires.push(last.at[beyond, pl.ds(side * rows, rows)], up_relay.at[side], up(step))
        for side, step in ((0, 1), (1, -1))
    ]
    up_lands = []
    for side, step in ((0, 1), (1, -1)):
        up_turns[side].wait_recv()
        beside = wrap(z + step)
        part = pl.ds(side * rows, rows)
        total = last[beside, part].astype(jnp.float32) + up_relay[side].astype(jnp.float32)
        last[beside, part] = total.astype(jnp.bfloat16)
        up_lands.append(wires.push(last.at[beside], up_land.at[side], up(step)))
    for copy in up_lands:
        copy.wait_recv()
    total = last[z].astype(jnp.float32)
    total = total + up_land[0].astype(jnp.float32) + up_land[1].astype(jnp.float32)
    last[z] = total.astype(jnp.bfloat16)
    copy = wires.push(last.at[z, span(1 - low)], twin_land, twin)
    copy.wait_recv()
    total = hidden[...] + last[z, span(low)].astype(jnp.float32)
    final[...] = (total + twin_land[...].astype(jnp.float32)).astype(jnp.bfloat16)

    local = pltpu.make_async_copy(final, out.at[y * 2 + low], local_sems.at[0])
    local.start()
    results = [wires.push(final, out.at[y * 2 + low], peer) for peer in peers]
    local.wait()
    for copy in results:
        copy.wait_recv()
    wires.drain()


def mixture(mine, hidden, gate_weight, up_weight, down_weight):
    rows, columns = mine.shape
    features = hidden.shape[1]
    here, _, width = gate_weight.shape
    two = 2 * rows
    kind = mine.dtype
    copies = 1 + 4 + 4 + 8 + 4 + 16 + 16 + 16 + 4 + 4 + 1 + 7
    grain = (RING, two, features)
    halves = (2, two, features)
    scratch = lambda *shape: pltpu.VMEM(shape, kind)
    anywhere = pl.BlockSpec(memory_space=pl.ANY)
    inside = pl.BlockSpec(memory_space=pltpu.VMEM)
    return pl.pallas_call(
        mixture_kernel,
        out_shape=jax.ShapeDtypeStruct((8, rows, features), kind),
        in_specs=[inside, inside, anywhere, anywhere, anywhere],
        out_specs=anywhere,
        scratch_shapes=[
            scratch(RING, RING, 2, RING, two, columns),
            scratch(16, *grain),
            scratch(16, *grain),
            scratch(16, *grain),
            scratch(RING, 2, *halves),
            scratch(RING, 2, *grain),
            scratch(2, *halves),
            scratch(2, *grain),
            scratch(2, rows, features),
            scratch(2, two, features),
            scratch(rows, features),
            scratch(rows, features),
            scratch(features, 2 * here * width),
            scratch(here * width, features),
            pltpu.SemaphoreType.DMA((copies,)),
            pltpu.SemaphoreType.DMA((copies,)),
            pltpu.SemaphoreType.DMA((1 + 3 * here,)),
        ],
        compiler_params=pltpu.CompilerParams(
            collective_id=1, has_side_effects=True, vmem_limit_bytes=62 * 1024 * 1024
        ),
        name="mixture",
    )(mine, hidden, gate_weight, up_weight, down_weight).reshape(8 * rows, features)


def pages_kernel(blocks, kv, keys, values):
    columns = keys.shape[-1]
    keys[...] = kv[:, :, :columns]
    values[...] = kv[:, :, columns:]


def write_pages(kv, blocks, columns):
    count = blocks.shape[0]
    out = jax.ShapeDtypeStruct((count, PAGE, columns), kv.dtype)
    spec = pl.BlockSpec((1, PAGE, columns), lambda j, blocks: (j, 0, 0))
    return pl.pallas_call(
        pages_kernel,
        out_shape=(out, out),
        grid_spec=pltpu.PrefetchScalarGridSpec(
            num_scalar_prefetch=1,
            grid=(count,),
            in_specs=[pl.BlockSpec((1, PAGE, 2 * columns), lambda j, blocks: (blocks[j], 0, 0))],
            out_specs=(spec, spec),
        ),
        name="write_pages",
    )(blocks, kv.reshape(-1, PAGE, 2 * columns))


def rms_scale(matrix, scaling):
    mean_square = jnp.mean(matrix * matrix, axis=-1, keepdims=True)
    return matrix * lax.rsqrt(mean_square + epsilon) * scaling


def segment_info(lengths, places):
    starts = jnp.cumsum(lengths) - lengths
    inside = (places[:, None] >= starts[None, :]).astype(jnp.int32)
    segment = jnp.sum(inside, axis=1) - 1
    slot_ids = jnp.arange(starts.shape[0], dtype=jnp.int32)
    seg_start = jnp.sum(
        jnp.where(slot_ids[None, :] == segment[:, None], starts[None, :], 0), axis=1
    )
    return (segment, places - seg_start)


def rotate(matrix, position):
    half_dim = matrix.shape[-1] // 2
    frequency = jnp.exp(
        -jnp.log(rope_base) * jnp.arange(half_dim, dtype=jnp.float32) * (2.0 / matrix.shape[-1])
    )
    angles = position.astype(jnp.float32)[:, None] * frequency[None, :]
    cosine = jnp.cos(angles)[:, None, :]
    sine_part = jnp.sin(angles)[:, None, :]
    first_half = matrix[..., :half_dim]
    second = matrix[..., half_dim:]
    return jnp.concatenate(
        [first_half * cosine - second * sine_part, second * cosine + first_half * sine_part],
        axis=-1,
    )


def local(
    tokens,
    lengths,
    page_table,
    attention_gain,
    query_weight,
    key_weight,
    value_weight,
    out_weight,
    expert_gain,
    router_weight,
    expert_ids,
    gate_weight,
    up_weight,
    down_weight,
):
    row_count = tokens.shape[0]
    feature_count = tokens.shape[1]
    span_size = query_weight.shape[1]
    head_count = span_size // HEAD_DIM
    shard_id = lax.axis_index("seq")
    places = shard_id * row_count + jnp.arange(row_count, dtype=jnp.int32)
    segment, position = segment_info(lengths, places)
    stream = tokens.astype(jnp.float32)
    normed = rms_scale(stream, attention_gain).astype(jnp.bfloat16)

    def project(weight):
        return jnp.dot(normed, weight, preferred_element_type=jnp.float32)

    def turned(matrix):
        return rotate(matrix.reshape(row_count, head_count, HEAD_DIM), position).astype(
            jnp.bfloat16
        )

    key_rows = turned(project(key_weight)).reshape(row_count, span_size)
    value_rows = project(value_weight).astype(jnp.bfloat16)
    kv = gather_stream(jnp.concatenate([key_rows, value_rows], axis=1))
    queries = turned(project(query_weight))

    page_rows = row_count // PAGE
    my_pages = shard_id * page_rows + jnp.arange(page_rows, dtype=jnp.int32)
    block_ids = jnp.arange(page_table.shape[0], dtype=jnp.int32)
    blocks = jnp.sum(
        jnp.where(page_table[None, :] == my_pages[:, None], block_ids[None, :], 0), axis=1
    )
    key_cache, value_cache = write_pages(kv, blocks, span_size)

    piece_rows = kv.shape[0]
    key_places = jnp.arange(piece_rows, dtype=jnp.int32)
    key_segments, _ = segment_info(lengths, key_places)
    scores = jnp.einsum(
        "qhd,khd->hqk",
        queries,
        kv[:, :span_size].reshape(piece_rows, head_count, HEAD_DIM),
        preferred_element_type=jnp.float32,
    ) * (HEAD_DIM ** (-0.5))
    allowed = (
        (segment[:, None] == key_segments[None, :]) & (key_places[None, :] <= places[:, None])
    )[None]
    peak = jnp.max(jnp.where(allowed, scores, -1e30), axis=-1)
    raised = jnp.where(allowed, jnp.exp(scores - peak[:, :, None]), 0.0)
    row_total = jnp.sum(raised, axis=-1)
    weighted = jnp.einsum(
        "hqk,khd->hqd",
        raised.astype(jnp.bfloat16),
        kv[:, span_size:].reshape(piece_rows, head_count, HEAD_DIM),
        preferred_element_type=jnp.float32,
    )
    attended = (
        jnp.transpose(weighted / row_total[:, :, None], (1, 0, 2))
        .reshape(row_count, span_size)
        .astype(jnp.bfloat16)
    )
    head_part = jnp.dot(attended, out_weight, preferred_element_type=jnp.float32)

    member = lax.axis_index("tensor")
    own_rows = row_count // lax.axis_size("tensor")
    own_stream = lax.dynamic_slice_in_dim(tokens, member * own_rows, own_rows, 0)
    own_ids = lax.dynamic_slice_in_dim(expert_ids, member * own_rows, own_rows, 0)
    hidden = own_stream.astype(jnp.float32) + scatter_tensor(head_part.astype(jnp.bfloat16))
    moe_input = rms_scale(hidden, expert_gain).astype(jnp.bfloat16)
    expert_count = router_weight.shape[1]
    probability = jax.nn.softmax(
        jnp.dot(moe_input, router_weight, preferred_element_type=jnp.float32), axis=-1
    )
    expert_range = jnp.arange(expert_count, dtype=jnp.int32)
    named = jnp.any(own_ids[:, :, None] == expert_range[None, None, :], axis=1)
    share = jnp.where(named, probability, 0.0)
    share_high = share.astype(jnp.bfloat16)
    share_low = (share - share_high.astype(jnp.float32)).astype(jnp.bfloat16)

    mine = jnp.concatenate([moe_input, share_high, share_low], axis=1)
    layer_out = mixture(mine, hidden, gate_weight, up_weight, down_weight)
    return (layer_out, key_cache, value_cache)


def solution(mesh):
    return jax.shard_map(
        local,
        mesh=mesh,
        in_specs=(
            P("seq", None),
            P(),
            P(),
            P(),
            P(None, "tensor"),
            P(None, "tensor"),
            P(None, "tensor"),
            P("tensor", None),
            P(),
            P(),
            P("seq", None),
            P("seq", None, "tensor"),
            P("seq", None, "tensor"),
            P("seq", "tensor", None),
        ),
        out_specs=(P("seq", None), P("seq", None, "tensor"), P("seq", None, "tensor")),
        check_vma=False,
    )
```

```python
import functools

import jax
import jax.numpy as jnp
from jax import lax
from jax.experimental import pallas as pl
from jax.experimental.pallas import tpu as pltpu
from jax.sharding import PartitionSpec as P

HEAD_DIM = 128
PAGE = 16
RING = 4
BATCH = 2
MESH = pl.DeviceIdType.MESH

epsilon = 1e-05
rope_base = 10000.0


def place():
    seq = lax.axis_index("seq")
    tensor = lax.axis_index("tensor")
    return seq // 8, (seq // 2) % RING, seq % 2, tensor // 2, tensor % 2


def device(z, x, core, y, low):
    z, x, y = (z + RING) % RING, (x + RING) % RING, (y + RING) % RING
    return ((z * RING + x) * 2 + core, y * 2 + low)


def greet(peers):
    barrier = pltpu.get_barrier_semaphore()
    for peer in peers:
        pl.semaphore_signal(barrier, inc=1, device_id=peer, device_id_type=MESH)
    pl.semaphore_wait(barrier, len(peers))


class Wires:
    def __init__(self, send_sems, recv_sems):
        self.send_sems, self.recv_sems, self.copies = send_sems, recv_sems, []

    def push(self, source, target, peer):
        number = len(self.copies)
        copy = pltpu.make_async_remote_copy(
            src_ref=source,
            dst_ref=target,
            send_sem=self.send_sems.at[number],
            recv_sem=self.recv_sems.at[number],
            device_id=peer,
            device_id_type=MESH,
        )
        copy.start()
        self.copies.append(copy)
        return copy

    def drain(self):
        for copy in self.copies:
            copy.wait_send()


def tensor_peers():
    seq, tensor = lax.axis_index("seq"), lax.axis_index("tensor")
    return [(seq, (tensor + step) % 8) for step in range(1, 8)]


def attend_kernel(
    blocks, mine, normed, query_weight, cosine, sine, first, out_weight, own_stream,
    hidden, key_pages, value_pages,
    kv, parts, landed, queries, peak, total, weighted,
    send_sems, recv_sems, local_sem,
):
    z, x, core, y, low = place()
    near = lambda step: device(z + step, x, core, y, low)
    far = lambda step: device(z, x + step, core, y, low)
    mate = device(z, x, 1 - core, y, low)
    peers = tensor_peers()
    greet([near(1), near(-1), far(1), far(-1), mate] + peers)
    wires = Wires(send_sems, recv_sems)
    rows = normed.shape[0]
    page_rows = rows // PAGE
    span_size = query_weight.shape[1]
    heads = span_size // HEAD_DIM

    def wrap(v):
        return (v + RING) % RING

    local = pltpu.make_async_copy(mine, kv.at[core, x, z], local_sem)
    local.start()
    local.wait()

    mates = []

    def share(z_at, x_at):
        piece = kv.at[core, x_at, z_at]
        mates.append(wires.push(piece, piece, mate))

    def across(z_at):
        piece = kv.at[core, x, z_at]
        ahead = wires.push(piece, piece, far(1))
        back = wires.push(piece, piece, far(-1))
        share(z_at, x)
        return ahead, back

    half = page_rows // 2
    own = kv.at[core, x, z]
    ahead = wires.push(own, own, near(1))
    back = wires.push(own, own, near(-1))
    origins = [z, wrap(z - 1), wrap(z + 1), wrap(z + 2)]
    pairs = [across(origins[0])]

    product = jnp.dot(normed[...], query_weight[...], preferred_element_type=jnp.float32)
    for head in range(heads):
        one = product[:, head * HEAD_DIM : (head + 1) * HEAD_DIM]
        one = one * cosine[...] + pltpu.roll(one, HEAD_DIM // 2, 1) * sine[...]
        queries[head] = one.astype(jnp.bfloat16)
    peak[...] = jnp.full(peak.shape, -1e30, jnp.float32)
    total[...] = jnp.zeros(total.shape, jnp.float32)
    weighted[...] = jnp.zeros(weighted.shape, jnp.float32)

    ahead.wait_recv()
    piece = kv.at[core, x, origins[1], pl.ds(0, half)]
    ahead = wires.push(piece, piece, near(1))
    pairs.append(across(origins[1]))
    back.wait_recv()
    piece = kv.at[core, x, origins[2], pl.ds(half, half)]
    back = wires.push(piece, piece, near(-1))
    pairs.append(across(origins[2]))
    ahead.wait_recv()
    back.wait_recv()
    pairs.append(across(origins[3]))
    relays = []

    def onward(number):
        ahead, back = pairs[number]
        ahead.wait_recv()
        if number < 2:
            piece = kv.at[core, wrap(x - 1), origins[number]]
            relays.append(wires.push(piece, piece, far(1)))
        share(origins[number], wrap(x - 1))
        back.wait_recv()
        if number >= 2:
            piece = kv.at[core, wrap(x + 1), origins[number]]
            relays.append(wires.push(piece, piece, far(-1)))
        share(origins[number], wrap(x + 1))

    start_at = first[...]
    here = lax.axis_index("seq") * rows + lax.broadcasted_iota(jnp.int32, (rows, 1), 0)
    keys_in = RING * rows

    def attend(side, x_at):
        line = kv[side, x_at].reshape(keys_in, 2 * span_size)
        column = lax.broadcasted_iota(jnp.int32, (1, keys_in), 1)
        at = ((column // rows * RING + x_at) * 2 + side) * rows + column % rows
        allowed = (at >= start_at) & (at <= here)
        for head in range(heads):
            keys = line[:, head * HEAD_DIM : (head + 1) * HEAD_DIM]
            values = line[:, span_size + head * HEAD_DIM : span_size + (head + 1) * HEAD_DIM]
            scores = lax.dot_general(
                queries[head], keys, (((1,), (1,)), ((), ())), preferred_element_type=jnp.float32
            ) * (HEAD_DIM ** (-0.5))
            old = peak[head]
            new = jnp.maximum(
                old, jnp.max(jnp.where(allowed, scores, -1e30), axis=1, keepdims=True)
            )
            raised = jnp.where(allowed, jnp.exp(scores - new[:, :1]), 0.0)
            keep = jnp.exp(old - new)
            total[head] = total[head] * keep + jnp.sum(raised, axis=1, keepdims=True)
            weighted[head] = weighted[head] * keep + jnp.dot(
                raised.astype(jnp.bfloat16), values, preferred_element_type=jnp.float32
            )
            peak[head] = new

    def arrived(numbers):
        for number in numbers:
            mates[number].wait_recv()

    onward(0)
    attend(core, x)
    onward(1)
    arrived((0, 1, 2, 3))
    attend(1 - core, x)
    onward(2)
    onward(3)
    attend(core, wrap(x - 1))
    attend(core, wrap(x + 1))
    relays[0].wait_recv()
    share(origins[0], wrap(x + 2))
    relays[1].wait_recv()
    share(origins[1], wrap(x + 2))
    arrived((4, 6, 8, 10))
    attend(1 - core, wrap(x - 1))
    relays[2].wait_recv()
    share(origins[2], wrap(x + 2))
    relays[3].wait_recv()
    share(origins[3], wrap(x + 2))
    arrived((5, 7, 9, 11))
    attend(1 - core, wrap(x + 1))
    attend(core, wrap(x + 2))
    arrived((12, 13, 14, 15))
    attend(1 - core, wrap(x + 2))

    attended = jnp.concatenate(
        [(weighted[head] / total[head]).astype(jnp.bfloat16) for head in range(heads)], axis=1
    )
    product = jnp.dot(attended, out_weight[...], preferred_element_type=jnp.float32)
    parts[...] = product.astype(jnp.bfloat16).reshape(parts.shape)
    sums = [
        wires.push(parts.at[peer[1]], landed.at[number], peer) for number, peer in enumerate(peers)
    ]

    for j in range(key_pages.shape[0]):
        block = blocks[j]
        shard = block // page_rows
        page = kv[shard % 2, (shard // 2) % RING, shard // (2 * RING), block % page_rows]
        key_pages[j] = page[:, :span_size]
        value_pages[j] = page[:, span_size:]

    result = own_stream[...] + parts[lax.axis_index("tensor")].astype(jnp.float32)
    for number, copy in enumerate(sums):
        copy.wait_recv()
        result = result + landed[number].astype(jnp.float32)
    hidden[...] = result
    wires.drain()


def attention(blocks, mine, normed, query_weight, cosine, sine, first, out_weight, own_stream):
    rows, columns = mine.shape
    own_rows, features = own_stream.shape
    heads = columns // (2 * HEAD_DIM)
    page_rows = rows // PAGE
    copies = 4 + 8 + 4 + 16 + 7
    inside = pl.BlockSpec(memory_space=pltpu.VMEM)
    pages = jax.ShapeDtypeStruct((page_rows, PAGE, columns // 2), mine.dtype)
    state = pltpu.VMEM((heads, rows, HEAD_DIM), jnp.float32)
    return pl.pallas_call(
        attend_kernel,
        out_shape=(jax.ShapeDtypeStruct((own_rows, features), jnp.float32), pages, pages),
        in_specs=[pl.BlockSpec(memory_space=pltpu.SMEM)] + [inside] * 8,
        out_specs=(inside, inside, inside),
        scratch_shapes=[
            pltpu.VMEM((2, RING, RING, page_rows, PAGE, columns), mine.dtype),
            pltpu.VMEM((8, own_rows, features), mine.dtype),
            pltpu.VMEM((7, own_rows, features), mine.dtype),
            pltpu.VMEM((heads, rows, HEAD_DIM), mine.dtype),
            state,
            state,
            state,
            pltpu.SemaphoreType.DMA((copies,)),
            pltpu.SemaphoreType.DMA((copies,)),
            pltpu.SemaphoreType.DMA,
        ],
        compiler_params=pltpu.CompilerParams(
            collective_id=0, has_side_effects=True, vmem_limit_bytes=40 * 1024 * 1024
        ),
        name="attention",
    )(
        blocks, mine.reshape(page_rows, PAGE, columns), normed, query_weight, cosine, sine, first,
        out_weight, own_stream,
    )

def mixture_kernel(
    mine, hidden, gate, up_part, down, out, rows_all, held, outbox, pair, near_relay, near_land,
    far_relay, far_land, up_relay, up_land, twin_land, final, weight_in, weight_out,
    send_sems, recv_sems, local_sems,
):
    z, x, core, y, low = place()
    up = lambda step: device(z + step, x, core, y, low)
    twin = device(z, x, core, y, 1 - low)
    near = lambda step: device(z, x + step * (1 - core), core, y + step * core, low)
    far = lambda step: device(z, x + step * core, core, y + step * (1 - core), low)
    mate = device(z, x, 1 - core, y, low)
    a, b = x * (1 - core) + y * core, y * (1 - core) + x * core
    peers = tensor_peers()
    ring_y = [near(1), near(-1), far(1), far(-1)]
    greet([up(1), up(-1), mate] + ring_y + peers)
    wires = Wires(send_sems, recv_sems)
    features, width = down.shape[2], gate.shape[2]
    experts_here = gate.shape[0]
    rows = mine.shape[0]

    span = lambda member: pl.ds(pl.multiple_of(member * rows, rows), rows)
    place_own = rows_all.at[core, b, a, z, span(low)]
    loads = [pltpu.make_async_copy(mine, place_own, local_sems.at[0])]
    for number in range(experts_here):
        for kind, source in enumerate((gate, up_part)):
            column = (kind * experts_here + number) * width
            loads.append(
                pltpu.make_async_copy(
                    source.at[number],
                    weight_in.at[:, pl.ds(column, width)],
                    local_sems.at[len(loads)],
                )
            )
        loads.append(
            pltpu.make_async_copy(
                down.at[number],
                weight_out.at[pl.ds(number * width, width)],
                local_sems.at[len(loads)],
            )
        )
    for load in loads:
        load.start()

    def wrap(v):
        return (v + RING) % RING

    def view(side, a_at, b_at, first=0, count=RING):
        return rows_all.at[side, b_at, a_at, pl.ds(first, count)]

    copy = wires.push(mine, place_own, twin)
    loads[0].wait()
    copy.wait_recv()
    both = rows_all.at[core, b, a, z]
    ahead = wires.push(both, both, up(1))
    back = wires.push(both, both, up(-1))
    ahead.wait_recv()
    piece = rows_all.at[core, b, a, wrap(z - 1), pl.ds(0, rows)]
    ahead = wires.push(piece, piece, up(1))
    back.wait_recv()
    piece = rows_all.at[core, b, a, wrap(z + 1), pl.ds(rows, rows)]
    back = wires.push(piece, piece, up(-1))
    ahead.wait_recv()
    back.wait_recv()

    mates = []

    def share(a_at, b_at):
        piece = view(core, a_at, b_at)
        mates.append(wires.push(piece, piece, mate))

    def across(a_at):
        piece = view(core, a_at, b)
        ahead = wires.push(piece, piece, far(1))
        back = wires.push(piece, piece, far(-1))
        share(a_at, b)
        return ahead, back

    own = view(core, a, b)
    ahead = wires.push(own, own, near(1))
    back = wires.push(own, own, near(-1))
    origins = [a, wrap(a - 1), wrap(a + 1), wrap(a + 2)]
    pairs = [across(origins[0])]
    ahead.wait_recv()
    piece = view(core, origins[1], b, 0, 2)
    ahead = wires.push(piece, piece, near(1))
    pairs.append(across(origins[1]))
    back.wait_recv()
    piece = view(core, origins[2], b, 2, 2)
    back = wires.push(piece, piece, near(-1))
    pairs.append(across(origins[2]))
    ahead.wait_recv()
    back.wait_recv()
    pairs.append(across(origins[3]))

    relays = []

    def onward(number):
        ahead, back = pairs[number]
        ahead.wait_recv()
        if number < 2:
            piece = view(core, origins[number], wrap(b - 1))
            relays.append(wires.push(piece, piece, far(1)))
        share(origins[number], wrap(b - 1))
        back.wait_recv()
        if number >= 2:
            piece = view(core, origins[number], wrap(b + 1))
            relays.append(wires.push(piece, piece, far(-1)))
        share(origins[number], wrap(b + 1))

    lines = (0, 3, 1, 2)
    first_expert = lax.axis_index("seq") * experts_here
    inner = experts_here * width

    def experts(side, line, target):
        b_at = (y * (1 - side) + x * side + lines[line]) % RING

        @pl.loop(0, RING // BATCH)
        def _(i):
            block = rows_all[side, b_at, pl.ds(i * BATCH, BATCH)]
            block = block.reshape(BATCH * RING * 2 * rows, block.shape[-1])
            product = jnp.dot(
                block[:, :features], weight_in[...], preferred_element_type=jnp.float32
            )
            shares = block[:, features:].astype(jnp.float32)
            names = lax.broadcasted_iota(jnp.int32, shares.shape, 1) % (shares.shape[1] // 2)
            scales = [
                jnp.broadcast_to(
                    jnp.sum(
                        jnp.where(names == first_expert + number, shares, 0.0),
                        axis=1,
                        keepdims=True,
                    ),
                    (shares.shape[0], width),
                )
                for number in range(experts_here)
            ]
            gated = product[:, :inner]
            active = gated / (1.0 + jnp.exp(-gated)) * product[:, inner:]
            active = (active * jnp.concatenate(scales, axis=1)).astype(jnp.bfloat16)
            term = jnp.dot(active, weight_out[...], preferred_element_type=jnp.float32)
            target[line, pl.ds(i * BATCH, BATCH)] = term.astype(jnp.bfloat16).reshape(
                BATCH, RING, 2 * rows, features
            )

    exchanges = {}

    def swap(line):
        for step in (2, 1, 3, 0):
            at = wrap(b + step)
            exchanges[line, step] = wires.push(outbox.at[line, at], pair.at[line, at], mate)

    def ours(line):
        experts(core, line, held)

    def theirs(line, numbers):
        for number in numbers:
            mates[number].wait_recv()
        experts(1 - core, line, outbox)
        swap(line)

    def add(target, first, count, sources):
        @pl.loop(0, count)
        def _(n):
            total = target[first + n].astype(jnp.float32)
            for source in sources:
                total = total + source[n].astype(jnp.float32)
            target[first + n] = total.astype(jnp.bfloat16)

    turns = {}
    lands = {}

    def opening(line):
        at = wrap(a + 2)
        exchanges[line, 2].wait_recv()
        add(held.at[line, at], 0, RING, [pair.at[line, at]])
        turns[line] = (
            wires.push(held.at[line, at, pl.ds(0, 2)], near_relay.at[line, 0], near(1)),
            wires.push(held.at[line, at, pl.ds(2, 2)], near_relay.at[line, 1], near(-1)),
        )

    def middle(line):
        for side, step in ((0, 1), (1, 3)):
            at = wrap(a + step)
            exchanges[line, step].wait_recv()
            piece, other = held.at[line, at], pair.at[line, at]
            add(piece, 2 - 2 * side, 2, [other.at[pl.ds(2 - 2 * side, 2)]])
            turns[line][side].wait_recv()
            add(piece, 2 * side, 2, [other.at[pl.ds(2 * side, 2)], near_relay.at[line, side]])
            lands[line, side] = wires.push(piece, near_land.at[line, side], near(1 - 2 * side))

    def closing(line):
        exchanges[line, 0].wait_recv()
        lands[line, 0].wait_recv()
        lands[line, 1].wait_recv()
        add(held.at[line, a], 0, RING, [pair.at[line, a], near_land.at[line, 0], near_land.at[line, 1]])

    def relayed(number):
        relays[number].wait_recv()
        share(origins[number], wrap(b + 2))

    onward(0)
    for load in loads[1:]:
        load.wait()
    ours(0)
    onward(1)
    theirs(0, (0, 1, 2, 3))
    onward(2)
    opening(0)
    onward(3)
    ours(1)
    middle(0)
    relayed(0)
    relayed(1)
    theirs(1, (4, 6, 8, 10))
    opening(1)
    closing(0)
    ours(2)
    relayed(2)
    relayed(3)
    middle(1)
    theirs(2, (5, 7, 9, 11))
    opening(2)
    closing(1)
    ours(3)
    middle(2)
    theirs(3, (12, 13, 14, 15))
    opening(3)
    closing(2)
    middle(3)
    closing(3)

    line_sum = lambda line: held.at[line, a]
    far_turns = (
        wires.push(held.at[3, a, pl.ds(0, 2)], far_relay.at[0], far(1)),
        wires.push(held.at[3, a, pl.ds(2, 2)], far_relay.at[1], far(-1)),
    )
    far_lands = []
    for side, line, step in ((0, 2, 1), (1, 1, -1)):
        far_turns[side].wait_recv()
        add(line_sum(line), 2 * side, 2, [far_relay.at[side]])
        far_lands.append(wires.push(line_sum(line), far_land.at[side], far(step)))
    for copy in far_lands:
        copy.wait_recv()
    last = line_sum(0)
    add(last, 0, RING, [far_land.at[0], far_land.at[1]])

    beyond = wrap(z + 2)
    up_turns = [
        wires.push(last.at[beyond, pl.ds(side * rows, rows)], up_relay.at[side], up(step))
        for side, step in ((0, 1), (1, -1))
    ]
    up_lands = []
    for side, step in ((0, 1), (1, -1)):
        up_turns[side].wait_recv()
        beside = wrap(z + step)
        part = pl.ds(side * rows, rows)
        total = last[beside, part].astype(jnp.float32) + up_relay[side].astype(jnp.float32)
        last[beside, part] = total.astype(jnp.bfloat16)
        up_lands.append(wires.push(last.at[beside], up_land.at[side], up(step)))
    for copy in up_lands:
        copy.wait_recv()
    total = last[z].astype(jnp.float32)
    total = total + up_land[0].astype(jnp.float32) + up_land[1].astype(jnp.float32)
    last[z] = total.astype(jnp.bfloat16)
    copy = wires.push(last.at[z, span(1 - low)], twin_land, twin)
    copy.wait_recv()
    total = hidden[...] + last[z, span(low)].astype(jnp.float32)
    final[...] = (total + twin_land[...].astype(jnp.float32)).astype(jnp.bfloat16)

    local = pltpu.make_async_copy(final, out.at[y * 2 + low], local_sems.at[0])
    local.start()
    results = [wires.push(final, out.at[y * 2 + low], peer) for peer in peers]
    local.wait()
    for copy in results:
        copy.wait_recv()
    wires.drain()


def mixture(mine, hidden, gate_weight, up_weight, down_weight):
    rows, columns = mine.shape
    features = hidden.shape[1]
    here, _, width = gate_weight.shape
    two = 2 * rows
    kind = mine.dtype
    copies = 1 + 4 + 4 + 8 + 4 + 16 + 16 + 16 + 4 + 4 + 1 + 7
    grain = (RING, two, features)
    halves = (2, two, features)
    scratch = lambda *shape: pltpu.VMEM(shape, kind)
    anywhere = pl.BlockSpec(memory_space=pl.ANY)
    inside = pl.BlockSpec(memory_space=pltpu.VMEM)
    return pl.pallas_call(
        mixture_kernel,
        out_shape=jax.ShapeDtypeStruct((8, rows, features), kind),
        in_specs=[inside, inside, anywhere, anywhere, anywhere],
        out_specs=anywhere,
        scratch_shapes=[
            scratch(2, RING, RING, RING, two, columns),
            scratch(RING, RING, *grain),
            scratch(RING, RING, *grain),
            scratch(RING, RING, *grain),
            scratch(RING, 2, *halves),
            scratch(RING, 2, *grain),
            scratch(2, *halves),
            scratch(2, *grain),
            scratch(2, rows, features),
            scratch(2, two, features),
            scratch(rows, features),
            scratch(rows, features),
            scratch(features, 2 * here * width),
            scratch(here * width, features),
            pltpu.SemaphoreType.DMA((copies,)),
            pltpu.SemaphoreType.DMA((copies,)),
            pltpu.SemaphoreType.DMA((1 + 3 * here,)),
        ],
        compiler_params=pltpu.CompilerParams(
            collective_id=1, has_side_effects=True, vmem_limit_bytes=62 * 1024 * 1024
        ),
        name="mixture",
    )(mine, hidden, gate_weight, up_weight, down_weight).reshape(8 * rows, features)


def rms_scale(matrix, scaling):
    mean_square = jnp.mean(matrix * matrix, axis=-1, keepdims=True)
    return matrix * lax.rsqrt(mean_square + epsilon) * scaling


def segment_info(lengths, places):
    starts = jnp.cumsum(lengths) - lengths
    inside = (places[:, None] >= starts[None, :]).astype(jnp.int32)
    segment = jnp.sum(inside, axis=1) - 1
    slot_ids = jnp.arange(starts.shape[0], dtype=jnp.int32)
    seg_start = jnp.sum(
        jnp.where(slot_ids[None, :] == segment[:, None], starts[None, :], 0), axis=1
    )
    return (segment, places - seg_start)


def rotate(matrix, position):
    half_dim = matrix.shape[-1] // 2
    frequency = jnp.exp(
        -jnp.log(rope_base) * jnp.arange(half_dim, dtype=jnp.float32) * (2.0 / matrix.shape[-1])
    )
    angles = position.astype(jnp.float32)[:, None] * frequency[None, :]
    cosine = jnp.cos(angles)[:, None, :]
    sine_part = jnp.sin(angles)[:, None, :]
    first_half = matrix[..., :half_dim]
    second = matrix[..., half_dim:]
    return jnp.concatenate(
        [first_half * cosine - second * sine_part, second * cosine + first_half * sine_part],
        axis=-1,
    )


def local(
    tokens,
    lengths,
    page_table,
    attention_gain,
    query_weight,
    key_weight,
    value_weight,
    out_weight,
    expert_gain,
    router_weight,
    expert_ids,
    gate_weight,
    up_weight,
    down_weight,
):
    row_count = tokens.shape[0]
    feature_count = tokens.shape[1]
    span_size = query_weight.shape[1]
    head_count = span_size // HEAD_DIM
    shard_id = lax.axis_index("seq")
    places = shard_id * row_count + jnp.arange(row_count, dtype=jnp.int32)
    segment, position = segment_info(lengths, places)
    stream = tokens.astype(jnp.float32)
    normed = rms_scale(stream, attention_gain).astype(jnp.bfloat16)

    def project(weight):
        return jnp.dot(normed, weight, preferred_element_type=jnp.float32)

    def turned(matrix):
        return rotate(matrix.reshape(row_count, head_count, HEAD_DIM), position).astype(
            jnp.bfloat16
        )

    key_rows = turned(project(key_weight)).reshape(row_count, span_size)
    value_rows = project(value_weight).astype(jnp.bfloat16)
    half_dim = HEAD_DIM // 2
    frequency = jnp.exp(
        -jnp.log(rope_base) * jnp.arange(half_dim, dtype=jnp.float32) * (2.0 / HEAD_DIM)
    )
    angles = position.astype(jnp.float32)[:, None] * frequency[None, :]
    cosine = jnp.concatenate([jnp.cos(angles), jnp.cos(angles)], axis=1)
    sine = jnp.concatenate([-jnp.sin(angles), jnp.sin(angles)], axis=1)

    page_rows = row_count // PAGE
    my_pages = shard_id * page_rows + jnp.arange(page_rows, dtype=jnp.int32)
    block_ids = jnp.arange(page_table.shape[0], dtype=jnp.int32)
    blocks = jnp.sum(
        jnp.where(page_table[None, :] == my_pages[:, None], block_ids[None, :], 0), axis=1
    )

    member = lax.axis_index("tensor")
    own_rows = row_count // lax.axis_size("tensor")
    own_stream = lax.dynamic_slice_in_dim(tokens, member * own_rows, own_rows, 0)
    own_ids = lax.dynamic_slice_in_dim(expert_ids, member * own_rows, own_rows, 0)
    hidden, key_cache, value_cache = attention(
        blocks,
        jnp.concatenate([key_rows, value_rows], axis=1),
        normed,
        query_weight,
        cosine,
        sine,
        (places - position)[:, None],
        out_weight,
        own_stream.astype(jnp.float32),
    )
    moe_input = rms_scale(hidden, expert_gain).astype(jnp.bfloat16)
    expert_count = router_weight.shape[1]
    probability = jax.nn.softmax(
        jnp.dot(moe_input, router_weight, preferred_element_type=jnp.float32), axis=-1
    )
    expert_range = jnp.arange(expert_count, dtype=jnp.int32)
    named = jnp.any(own_ids[:, :, None] == expert_range[None, None, :], axis=1)
    share = jnp.where(named, probability, 0.0)
    share_high = share.astype(jnp.bfloat16)
    share_low = (share - share_high.astype(jnp.float32)).astype(jnp.bfloat16)

    mine = jnp.concatenate([moe_input, share_high, share_low], axis=1)
    layer_out = mixture(mine, hidden, gate_weight, up_weight, down_weight)
    return (layer_out, key_cache, value_cache)


def solution(mesh):
    return jax.shard_map(
        local,
        mesh=mesh,
        in_specs=(
            P("seq", None),
            P(),
            P(),
            P(),
            P(None, "tensor"),
            P(None, "tensor"),
            P(None, "tensor"),
            P("tensor", None),
            P(),
            P(),
            P("seq", None),
            P("seq", None, "tensor"),
            P("seq", None, "tensor"),
            P("seq", "tensor", None),
        ),
        out_specs=(P("seq", None), P("seq", None, "tensor"), P("seq", None, "tensor")),
        check_vma=False,
    )
```

```python
import functools

import jax
import jax.numpy as jnp
from jax import lax
from jax.experimental import pallas as pl
from jax.experimental.pallas import tpu as pltpu
from jax.sharding import PartitionSpec as P

HEAD_DIM = 128
PAGE = 16
RING = 4
BATCH = 2
MESH = pl.DeviceIdType.MESH

epsilon = 1e-05
rope_base = 10000.0


def place():
    seq = lax.axis_index("seq")
    tensor = lax.axis_index("tensor")
    return seq // 8, (seq // 2) % RING, seq % 2, tensor // 2, tensor % 2


def device(z, x, core, y, low):
    z, x, y = (z + RING) % RING, (x + RING) % RING, (y + RING) % RING
    return ((z * RING + x) * 2 + core, y * 2 + low)


def greet(peers):
    barrier = pltpu.get_barrier_semaphore()
    for peer in peers:
        pl.semaphore_signal(barrier, inc=1, device_id=peer, device_id_type=MESH)
    pl.semaphore_wait(barrier, len(peers))


class Wires:
    def __init__(self, send_sems, recv_sems):
        self.send_sems, self.recv_sems, self.copies = send_sems, recv_sems, []

    def push(self, source, target, peer):
        number = len(self.copies)
        copy = pltpu.make_async_remote_copy(
            src_ref=source,
            dst_ref=target,
            send_sem=self.send_sems.at[number],
            recv_sem=self.recv_sems.at[number],
            device_id=peer,
            device_id_type=MESH,
        )
        copy.start()
        self.copies.append(copy)
        return copy

    def drain(self):
        for copy in self.copies:
            copy.wait_send()


def tensor_peers():
    seq, tensor = lax.axis_index("seq"), lax.axis_index("tensor")
    return [(seq, (tensor + step) % 8) for step in range(1, 8)]


def attend_kernel(
    blocks, mine, normed, query_weight, cosine, sine, first, out_weight, own_stream,
    hidden, key_pages, value_pages,
    kv, parts, landed, queries, peak, total, weighted,
    send_sems, recv_sems, local_sem,
):
    z, x, core, y, low = place()
    near = lambda step: device(z + step, x, core, y, low)
    far = lambda step: device(z, x + step, core, y, low)
    mate = device(z, x, 1 - core, y, low)
    peers = tensor_peers()
    greet([near(1), near(-1), far(1), far(-1), mate] + peers)
    wires = Wires(send_sems, recv_sems)
    rows = normed.shape[0]
    page_rows = rows // PAGE
    span_size = query_weight.shape[1]
    heads = span_size // HEAD_DIM

    def wrap(v):
        return (v + RING) % RING

    local = pltpu.make_async_copy(mine, kv.at[core, x, z], local_sem)
    local.start()
    local.wait()

    mates = []

    def share(z_at, x_at):
        piece = kv.at[core, x_at, z_at]
        mates.append(wires.push(piece, piece, mate))

    def across(z_at):
        piece = kv.at[core, x, z_at]
        ahead = wires.push(piece, piece, far(1))
        back = wires.push(piece, piece, far(-1))
        share(z_at, x)
        return ahead, back

    half = page_rows // 2
    own = kv.at[core, x, z]
    ahead = wires.push(own, own, near(1))
    back = wires.push(own, own, near(-1))
    origins = [z, wrap(z - 1), wrap(z + 1), wrap(z + 2)]
    pairs = [across(origins[0])]

    product = jnp.dot(normed[...], query_weight[...], preferred_element_type=jnp.float32)
    for head in range(heads):
        one = product[:, head * HEAD_DIM : (head + 1) * HEAD_DIM]
        one = one * cosine[...] + pltpu.roll(one, HEAD_DIM // 2, 1) * sine[...]
        queries[head] = one.astype(jnp.bfloat16)
    peak[...] = jnp.full(peak.shape, -1e30, jnp.float32)
    total[...] = jnp.zeros(total.shape, jnp.float32)
    weighted[...] = jnp.zeros(weighted.shape, jnp.float32)

    ahead.wait_recv()
    piece = kv.at[core, x, origins[1], pl.ds(0, half)]
    ahead = wires.push(piece, piece, near(1))
    pairs.append(across(origins[1]))
    back.wait_recv()
    piece = kv.at[core, x, origins[2], pl.ds(half, half)]
    back = wires.push(piece, piece, near(-1))
    pairs.append(across(origins[2]))
    ahead.wait_recv()
    back.wait_recv()
    pairs.append(across(origins[3]))
    relays = []

    def onward(number):
        ahead, back = pairs[number]
        ahead.wait_recv()
        if number < 2:
            piece = kv.at[core, wrap(x - 1), origins[number]]
            relays.append(wires.push(piece, piece, far(1)))
        share(origins[number], wrap(x - 1))
        back.wait_recv()
        if number >= 2:
            piece = kv.at[core, wrap(x + 1), origins[number]]
            relays.append(wires.push(piece, piece, far(-1)))
        share(origins[number], wrap(x + 1))

    start_at = first[...]
    here = lax.axis_index("seq") * rows + lax.broadcasted_iota(jnp.int32, (rows, 1), 0)
    keys_in = RING * rows

    def attend(side, x_at):
        line = kv[side, x_at].reshape(keys_in, 2 * span_size)
        column = lax.broadcasted_iota(jnp.int32, (1, keys_in), 1)
        at = ((column // rows * RING + x_at) * 2 + side) * rows + column % rows
        allowed = (at >= start_at) & (at <= here)
        for head in range(heads):
            keys = line[:, head * HEAD_DIM : (head + 1) * HEAD_DIM]
            values = line[:, span_size + head * HEAD_DIM : span_size + (head + 1) * HEAD_DIM]
            scores = lax.dot_general(
                queries[head], keys, (((1,), (1,)), ((), ())), preferred_element_type=jnp.float32
            ) * (HEAD_DIM ** (-0.5))
            old = peak[head]
            new = jnp.maximum(
                old, jnp.max(jnp.where(allowed, scores, -1e30), axis=1, keepdims=True)
            )
            raised = jnp.where(allowed, jnp.exp(scores - new[:, :1]), 0.0)
            keep = jnp.exp(old - new)
            total[head] = total[head] * keep + jnp.sum(raised, axis=1, keepdims=True)
            weighted[head] = weighted[head] * keep + jnp.dot(
                raised.astype(jnp.bfloat16), values, preferred_element_type=jnp.float32
            )
            peak[head] = new

    def arrived(numbers):
        for number in numbers:
            mates[number].wait_recv()

    onward(0)
    attend(core, x)
    onward(1)
    arrived((0, 1, 2, 3))
    attend(1 - core, x)
    onward(2)
    onward(3)
    attend(core, wrap(x - 1))
    attend(core, wrap(x + 1))
    relays[0].wait_recv()
    share(origins[0], wrap(x + 2))
    relays[1].wait_recv()
    share(origins[1], wrap(x + 2))
    arrived((4, 6, 8, 10))
    attend(1 - core, wrap(x - 1))
    relays[2].wait_recv()
    share(origins[2], wrap(x + 2))
    relays[3].wait_recv()
    share(origins[3], wrap(x + 2))
    arrived((5, 7, 9, 11))
    attend(1 - core, wrap(x + 1))
    attend(core, wrap(x + 2))
    arrived((12, 13, 14, 15))
    attend(1 - core, wrap(x + 2))

    attended = jnp.concatenate(
        [(weighted[head] / total[head]).astype(jnp.bfloat16) for head in range(heads)], axis=1
    )
    product = jnp.dot(attended, out_weight[...], preferred_element_type=jnp.float32)
    parts[...] = product.astype(jnp.bfloat16).reshape(parts.shape)
    sums = [
        wires.push(parts.at[peer[1]], landed.at[number], peer) for number, peer in enumerate(peers)
    ]

    for j in range(key_pages.shape[0]):
        block = blocks[j]
        shard = block // page_rows
        page = kv[shard % 2, (shard // 2) % RING, shard // (2 * RING), block % page_rows]
        key_pages[j] = page[:, :span_size]
        value_pages[j] = page[:, span_size:]

    result = own_stream[...] + parts[lax.axis_index("tensor")].astype(jnp.float32)
    for number, copy in enumerate(sums):
        copy.wait_recv()
        result = result + landed[number].astype(jnp.float32)
    hidden[...] = result
    wires.drain()


def attention(blocks, mine, normed, query_weight, cosine, sine, first, out_weight, own_stream):
    rows, columns = mine.shape
    own_rows, features = own_stream.shape
    heads = columns // (2 * HEAD_DIM)
    page_rows = rows // PAGE
    copies = 4 + 8 + 4 + 16 + 7
    inside = pl.BlockSpec(memory_space=pltpu.VMEM)
    pages = jax.ShapeDtypeStruct((page_rows, PAGE, columns // 2), mine.dtype)
    state = pltpu.VMEM((heads, rows, HEAD_DIM), jnp.float32)
    return pl.pallas_call(
        attend_kernel,
        out_shape=(jax.ShapeDtypeStruct((own_rows, features), jnp.float32), pages, pages),
        in_specs=[pl.BlockSpec(memory_space=pltpu.SMEM)] + [inside] * 8,
        out_specs=(inside, inside, inside),
        scratch_shapes=[
            pltpu.VMEM((2, RING, RING, page_rows, PAGE, columns), mine.dtype),
            pltpu.VMEM((8, own_rows, features), mine.dtype),
            pltpu.VMEM((7, own_rows, features), mine.dtype),
            pltpu.VMEM((heads, rows, HEAD_DIM), mine.dtype),
            state,
            state,
            state,
            pltpu.SemaphoreType.DMA((copies,)),
            pltpu.SemaphoreType.DMA((copies,)),
            pltpu.SemaphoreType.DMA,
        ],
        compiler_params=pltpu.CompilerParams(
            collective_id=0, has_side_effects=True, vmem_limit_bytes=40 * 1024 * 1024
        ),
        name="attention",
    )(
        blocks, mine.reshape(page_rows, PAGE, columns), normed, query_weight, cosine, sine, first,
        out_weight, own_stream,
    )

def mixture_kernel(
    mine, hidden, gate, up_part, down, out, rows_all, held, outbox, pair, near_relay, near_land,
    far_relay, far_land, up_relay, up_land, twin_land, final, weight_in, weight_out,
    send_sems, recv_sems, local_sems,
):
    z, x, core, y, low = place()
    up = lambda step: device(z + step, x, core, y, low)
    twin = device(z, x, core, y, 1 - low)
    near = lambda step: device(z, x + step * (1 - core), core, y + step * core, low)
    far = lambda step: device(z, x + step * core, core, y + step * (1 - core), low)
    mate = device(z, x, 1 - core, y, low)
    a, b = x * (1 - core) + y * core, y * (1 - core) + x * core
    peers = tensor_peers()
    ring_y = [near(1), near(-1), far(1), far(-1)]
    greet([up(1), up(-1), mate] + ring_y + peers)
    wires = Wires(send_sems, recv_sems)
    features, width = down.shape[2], gate.shape[2]
    experts_here = gate.shape[0]
    rows = mine.shape[0]

    span = lambda member: pl.ds(pl.multiple_of(member * rows, rows), rows)
    place_own = rows_all.at[core, b, a, z, span(low)]
    loads = [pltpu.make_async_copy(mine, place_own, local_sems.at[0])]
    for number in range(experts_here):
        for kind, source in enumerate((gate, up_part)):
            column = (kind * experts_here + number) * width
            loads.append(
                pltpu.make_async_copy(
                    source.at[number],
                    weight_in.at[:, pl.ds(column, width)],
                    local_sems.at[len(loads)],
                )
            )
        loads.append(
            pltpu.make_async_copy(
                down.at[number],
                weight_out.at[pl.ds(number * width, width)],
                local_sems.at[len(loads)],
            )
        )
    for load in loads:
        load.start()

    def wrap(v):
        return (v + RING) % RING

    def view(side, a_at, b_at, first=0, count=RING):
        return rows_all.at[side, b_at, a_at, pl.ds(first, count)]

    copy = wires.push(mine, place_own, twin)
    loads[0].wait()
    copy.wait_recv()
    starts = [[], [], [], []]

    def launch(z_at):
        piece = rows_all.at[core, b, a, z_at]
        for bundle, peer in zip(starts, (near(1), near(-1), far(1), far(-1))):
            bundle.append(wires.push(piece, piece, peer))

    def wait_all(bundle):
        for copy in bundle:
            copy.wait_recv()

    both = rows_all.at[core, b, a, z]
    ahead = wires.push(both, both, up(1))
    back = wires.push(both, both, up(-1))
    launch(z)
    ahead.wait_recv()
    piece = rows_all.at[core, b, a, wrap(z - 1), pl.ds(0, rows)]
    ahead = wires.push(piece, piece, up(1))
    launch(wrap(z - 1))
    back.wait_recv()
    piece = rows_all.at[core, b, a, wrap(z + 1), pl.ds(rows, rows)]
    back = wires.push(piece, piece, up(-1))
    launch(wrap(z + 1))
    ahead.wait_recv()
    back.wait_recv()
    launch(wrap(z + 2))

    mates = []

    def share(a_at, b_at):
        piece = view(core, a_at, b_at)
        mates.append(wires.push(piece, piece, mate))

    def across(a_at):
        piece = view(core, a_at, b)
        ahead = wires.push(piece, piece, far(1))
        back = wires.push(piece, piece, far(-1))
        share(a_at, b)
        return [ahead], [back]

    origins = [a, wrap(a - 1), wrap(a + 1), wrap(a + 2)]
    share(a, b)
    pairs = [(starts[2], starts[3])]
    wait_all(starts[0])
    piece = view(core, origins[1], b, 0, 2)
    ahead = wires.push(piece, piece, near(1))
    pairs.append(across(origins[1]))
    wait_all(starts[1])
    piece = view(core, origins[2], b, 2, 2)
    back = wires.push(piece, piece, near(-1))
    pairs.append(across(origins[2]))
    ahead.wait_recv()
    back.wait_recv()
    pairs.append(across(origins[3]))

    relays = []

    def onward(number):
        ahead, back = pairs[number]
        wait_all(ahead)
        if number < 2:
            piece = view(core, origins[number], wrap(b - 1))
            relays.append(wires.push(piece, piece, far(1)))
        share(origins[number], wrap(b - 1))
        wait_all(back)
        if number >= 2:
            piece = view(core, origins[number], wrap(b + 1))
            relays.append(wires.push(piece, piece, far(-1)))
        share(origins[number], wrap(b + 1))

    lines = (0, 3, 1, 2)
    first_expert = lax.axis_index("seq") * experts_here
    inner = experts_here * width

    def experts(side, line, target):
        b_at = (y * (1 - side) + x * side + lines[line]) % RING

        @pl.loop(0, RING // BATCH)
        def _(i):
            block = rows_all[side, b_at, pl.ds(i * BATCH, BATCH)]
            block = block.reshape(BATCH * RING * 2 * rows, block.shape[-1])
            product = jnp.dot(
                block[:, :features], weight_in[...], preferred_element_type=jnp.float32
            )
            shares = block[:, features:].astype(jnp.float32)
            names = lax.broadcasted_iota(jnp.int32, shares.shape, 1) % (shares.shape[1] // 2)
            scales = [
                jnp.broadcast_to(
                    jnp.sum(
                        jnp.where(names == first_expert + number, shares, 0.0),
                        axis=1,
                        keepdims=True,
                    ),
                    (shares.shape[0], width),
                )
                for number in range(experts_here)
            ]
            gated = product[:, :inner]
            active = gated / (1.0 + jnp.exp(-gated)) * product[:, inner:]
            active = (active * jnp.concatenate(scales, axis=1)).astype(jnp.bfloat16)
            term = jnp.dot(active, weight_out[...], preferred_element_type=jnp.float32)
            target[line, pl.ds(i * BATCH, BATCH)] = term.astype(jnp.bfloat16).reshape(
                BATCH, RING, 2 * rows, features
            )

    exchanges = {}

    def swap(line):
        for step in (2, 1, 3, 0):
            at = wrap(b + step)
            exchanges[line, step] = wires.push(outbox.at[line, at], pair.at[line, at], mate)

    def ours(line):
        experts(core, line, held)

    def theirs(line, numbers):
        for number in numbers:
            mates[number].wait_recv()
        experts(1 - core, line, outbox)
        swap(line)

    def add(target, first, count, sources):
        @pl.loop(0, count)
        def _(n):
            total = target[first + n].astype(jnp.float32)
            for source in sources:
                total = total + source[n].astype(jnp.float32)
            target[first + n] = total.astype(jnp.bfloat16)

    turns = {}
    lands = {}

    def opening(line):
        at = wrap(a + 2)
        exchanges[line, 2].wait_recv()
        add(held.at[line, at], 0, RING, [pair.at[line, at]])
        turns[line] = (
            wires.push(held.at[line, at, pl.ds(0, 2)], near_relay.at[line, 0], near(1)),
            wires.push(held.at[line, at, pl.ds(2, 2)], near_relay.at[line, 1], near(-1)),
        )

    def middle(line):
        for side, step in ((0, 1), (1, 3)):
            at = wrap(a + step)
            exchanges[line, step].wait_recv()
            piece, other = held.at[line, at], pair.at[line, at]
            add(piece, 2 - 2 * side, 2, [other.at[pl.ds(2 - 2 * side, 2)]])
            turns[line][side].wait_recv()
            add(piece, 2 * side, 2, [other.at[pl.ds(2 * side, 2)], near_relay.at[line, side]])
            lands[line, side] = wires.push(piece, near_land.at[line, side], near(1 - 2 * side))

    def closing(line):
        exchanges[line, 0].wait_recv()
        lands[line, 0].wait_recv()
        lands[line, 1].wait_recv()
        add(held.at[line, a], 0, RING, [pair.at[line, a], near_land.at[line, 0], near_land.at[line, 1]])

    def relayed(number):
        relays[number].wait_recv()
        share(origins[number], wrap(b + 2))

    onward(0)
    for load in loads[1:]:
        load.wait()
    ours(0)
    onward(1)
    theirs(0, (0, 1, 2, 3))
    onward(2)
    onward(3)
    opening(0)
    ours(1)
    relayed(0)
    relayed(1)
    theirs(1, (4, 6, 8, 10))
    ours(2)
    relayed(2)
    relayed(3)
    opening(1)
    middle(0)
    theirs(2, (5, 7, 9, 11))
    ours(3)
    opening(2)
    theirs(3, (12, 13, 14, 15))
    opening(3)
    middle(1)
    middle(2)
    middle(3)
    closing(0)
    closing(1)
    closing(2)
    closing(3)

    line_sum = lambda line: held.at[line, a]
    far_turns = (
        wires.push(held.at[3, a, pl.ds(0, 2)], far_relay.at[0], far(1)),
        wires.push(held.at[3, a, pl.ds(2, 2)], far_relay.at[1], far(-1)),
    )
    for side, line in ((0, 2), (1, 1)):
        far_turns[side].wait_recv()
        add(line_sum(line), 2 * side, 2, [far_relay.at[side]])
    far_lands = {}
    for step in (2, 1, 3, 0):
        at = wrap(z + step)
        far_lands[step] = [
            wires.push(line_sum(line).at[at], far_land.at[side, at], far(1 - 2 * side))
            for side, line in ((0, 2), (1, 1))
        ]
    last = line_sum(0)

    def finish(step):
        at = wrap(z + step)
        wait_all(far_lands[step])
        add(last, at, 1, [far_land.at[0, pl.ds(at, 1)], far_land.at[1, pl.ds(at, 1)]])

    finish(2)
    beyond = wrap(z + 2)
    up_turns = [
        wires.push(last.at[beyond, pl.ds(side * rows, rows)], up_relay.at[side], up(step))
        for side, step in ((0, 1), (1, -1))
    ]
    up_lands = []
    for side, step in ((0, 1), (1, 3)):
        finish(step)
        up_turns[side].wait_recv()
        beside = wrap(z + step)
        part = pl.ds(side * rows, rows)
        total = last[beside, part].astype(jnp.float32) + up_relay[side].astype(jnp.float32)
        last[beside, part] = total.astype(jnp.bfloat16)
        up_lands.append(wires.push(last.at[beside], up_land.at[side], up(1 - 2 * side)))
    finish(0)
    for copy in up_lands:
        copy.wait_recv()
    total = last[z].astype(jnp.float32)
    total = total + up_land[0].astype(jnp.float32) + up_land[1].astype(jnp.float32)
    last[z] = total.astype(jnp.bfloat16)
    copy = wires.push(last.at[z, span(1 - low)], twin_land, twin)
    copy.wait_recv()
    total = hidden[...] + last[z, span(low)].astype(jnp.float32)
    final[...] = (total + twin_land[...].astype(jnp.float32)).astype(jnp.bfloat16)

    local = pltpu.make_async_copy(final, out.at[y * 2 + low], local_sems.at[0])
    local.start()
    results = [wires.push(final, out.at[y * 2 + low], peer) for peer in peers]
    local.wait()
    for copy in results:
        copy.wait_recv()
    wires.drain()


def mixture(mine, hidden, gate_weight, up_weight, down_weight):
    rows, columns = mine.shape
    features = hidden.shape[1]
    here, _, width = gate_weight.shape
    two = 2 * rows
    kind = mine.dtype
    copies = 1 + 4 + 16 + 2 + 6 + 4 + 16 + 16 + 16 + 10 + 4 + 1 + 7
    grain = (RING, two, features)
    halves = (2, two, features)
    scratch = lambda *shape: pltpu.VMEM(shape, kind)
    anywhere = pl.BlockSpec(memory_space=pl.ANY)
    inside = pl.BlockSpec(memory_space=pltpu.VMEM)
    return pl.pallas_call(
        mixture_kernel,
        out_shape=jax.ShapeDtypeStruct((8, rows, features), kind),
        in_specs=[inside, inside, anywhere, anywhere, anywhere],
        out_specs=anywhere,
        scratch_shapes=[
            scratch(2, RING, RING, RING, two, columns),
            scratch(RING, RING, *grain),
            scratch(RING, RING, *grain),
            scratch(RING, RING, *grain),
            scratch(RING, 2, *halves),
            scratch(RING, 2, *grain),
            scratch(2, *halves),
            scratch(2, *grain),
            scratch(2, rows, features),
            scratch(2, two, features),
            scratch(rows, features),
            scratch(rows, features),
            scratch(features, 2 * here * width),
            scratch(here * width, features),
            pltpu.SemaphoreType.DMA((copies,)),
            pltpu.SemaphoreType.DMA((copies,)),
            pltpu.SemaphoreType.DMA((1 + 3 * here,)),
        ],
        compiler_params=pltpu.CompilerParams(
            collective_id=1, has_side_effects=True, vmem_limit_bytes=62 * 1024 * 1024
        ),
        name="mixture",
    )(mine, hidden, gate_weight, up_weight, down_weight).reshape(8 * rows, features)


def rms_scale(matrix, scaling):
    mean_square = jnp.mean(matrix * matrix, axis=-1, keepdims=True)
    return matrix * lax.rsqrt(mean_square + epsilon) * scaling


def segment_info(lengths, places):
    starts = jnp.cumsum(lengths) - lengths
    inside = (places[:, None] >= starts[None, :]).astype(jnp.int32)
    segment = jnp.sum(inside, axis=1) - 1
    slot_ids = jnp.arange(starts.shape[0], dtype=jnp.int32)
    seg_start = jnp.sum(
        jnp.where(slot_ids[None, :] == segment[:, None], starts[None, :], 0), axis=1
    )
    return (segment, places - seg_start)


def rotate(matrix, position):
    half_dim = matrix.shape[-1] // 2
    frequency = jnp.exp(
        -jnp.log(rope_base) * jnp.arange(half_dim, dtype=jnp.float32) * (2.0 / matrix.shape[-1])
    )
    angles = position.astype(jnp.float32)[:, None] * frequency[None, :]
    cosine = jnp.cos(angles)[:, None, :]
    sine_part = jnp.sin(angles)[:, None, :]
    first_half = matrix[..., :half_dim]
    second = matrix[..., half_dim:]
    return jnp.concatenate(
        [first_half * cosine - second * sine_part, second * cosine + first_half * sine_part],
        axis=-1,
    )


def local(
    tokens,
    lengths,
    page_table,
    attention_gain,
    query_weight,
    key_weight,
    value_weight,
    out_weight,
    expert_gain,
    router_weight,
    expert_ids,
    gate_weight,
    up_weight,
    down_weight,
):
    row_count = tokens.shape[0]
    feature_count = tokens.shape[1]
    span_size = query_weight.shape[1]
    head_count = span_size // HEAD_DIM
    shard_id = lax.axis_index("seq")
    places = shard_id * row_count + jnp.arange(row_count, dtype=jnp.int32)
    segment, position = segment_info(lengths, places)
    stream = tokens.astype(jnp.float32)
    normed = rms_scale(stream, attention_gain).astype(jnp.bfloat16)

    def project(weight):
        return jnp.dot(normed, weight, preferred_element_type=jnp.float32)

    def turned(matrix):
        return rotate(matrix.reshape(row_count, head_count, HEAD_DIM), position).astype(
            jnp.bfloat16
        )

    key_rows = turned(project(key_weight)).reshape(row_count, span_size)
    value_rows = project(value_weight).astype(jnp.bfloat16)
    half_dim = HEAD_DIM // 2
    frequency = jnp.exp(
        -jnp.log(rope_base) * jnp.arange(half_dim, dtype=jnp.float32) * (2.0 / HEAD_DIM)
    )
    angles = position.astype(jnp.float32)[:, None] * frequency[None, :]
    cosine = jnp.concatenate([jnp.cos(angles), jnp.cos(angles)], axis=1)
    sine = jnp.concatenate([-jnp.sin(angles), jnp.sin(angles)], axis=1)

    page_rows = row_count // PAGE
    my_pages = shard_id * page_rows + jnp.arange(page_rows, dtype=jnp.int32)
    block_ids = jnp.arange(page_table.shape[0], dtype=jnp.int32)
    blocks = jnp.sum(
        jnp.where(page_table[None, :] == my_pages[:, None], block_ids[None, :], 0), axis=1
    )

    member = lax.axis_index("tensor")
    own_rows = row_count // lax.axis_size("tensor")
    own_stream = lax.dynamic_slice_in_dim(tokens, member * own_rows, own_rows, 0)
    own_ids = lax.dynamic_slice_in_dim(expert_ids, member * own_rows, own_rows, 0)
    hidden, key_cache, value_cache = attention(
        blocks,
        jnp.concatenate([key_rows, value_rows], axis=1),
        normed,
        query_weight,
        cosine,
        sine,
        (places - position)[:, None],
        out_weight,
        own_stream.astype(jnp.float32),
    )
    moe_input = rms_scale(hidden, expert_gain).astype(jnp.bfloat16)
    expert_count = router_weight.shape[1]
    probability = jax.nn.softmax(
        jnp.dot(moe_input, router_weight, preferred_element_type=jnp.float32), axis=-1
    )
    expert_range = jnp.arange(expert_count, dtype=jnp.int32)
    named = jnp.any(own_ids[:, :, None] == expert_range[None, None, :], axis=1)
    share = jnp.where(named, probability, 0.0)
    share_high = share.astype(jnp.bfloat16)
    share_low = (share - share_high.astype(jnp.float32)).astype(jnp.bfloat16)

    mine = jnp.concatenate([moe_input, share_high, share_low], axis=1)
    layer_out = mixture(mine, hidden, gate_weight, up_weight, down_weight)
    return (layer_out, key_cache, value_cache)


def solution(mesh):
    return jax.shard_map(
        local,
        mesh=mesh,
        in_specs=(
            P("seq", None),
            P(),
            P(),
            P(),
            P(None, "tensor"),
            P(None, "tensor"),
            P(None, "tensor"),
            P("tensor", None),
            P(),
            P(),
            P("seq", None),
            P("seq", None, "tensor"),
            P("seq", None, "tensor"),
            P("seq", "tensor", None),
        ),
        out_specs=(P("seq", None), P("seq", None, "tensor"), P("seq", None, "tensor")),
        check_vma=False,
    )
```

```python
import functools

import jax
import jax.numpy as jnp
from jax import lax
from jax.experimental import pallas as pl
from jax.experimental.pallas import tpu as pltpu
from jax.sharding import PartitionSpec as P

HEAD_DIM = 128
PAGE = 16
RING = 4
BATCH = 2
MESH = pl.DeviceIdType.MESH

epsilon = 1e-05
rope_base = 10000.0


def place():
    seq = lax.axis_index("seq")
    tensor = lax.axis_index("tensor")
    return seq // 8, (seq // 2) % RING, seq % 2, tensor // 2, tensor % 2


def device(z, x, core, y, low):
    z, x, y = (z + RING) % RING, (x + RING) % RING, (y + RING) % RING
    return ((z * RING + x) * 2 + core, y * 2 + low)


def greet(peers):
    barrier = pltpu.get_barrier_semaphore()
    for peer in peers:
        pl.semaphore_signal(barrier, inc=1, device_id=peer, device_id_type=MESH)
    pl.semaphore_wait(barrier, len(peers))


class Wires:
    def __init__(self, send_sems, recv_sems):
        self.send_sems, self.recv_sems, self.copies = send_sems, recv_sems, []

    def push(self, source, target, peer):
        number = len(self.copies)
        copy = pltpu.make_async_remote_copy(
            src_ref=source,
            dst_ref=target,
            send_sem=self.send_sems.at[number],
            recv_sem=self.recv_sems.at[number],
            device_id=peer,
            device_id_type=MESH,
        )
        copy.start()
        self.copies.append(copy)
        return copy

    def drain(self):
        for copy in self.copies:
            copy.wait_send()


def tensor_peers():
    seq, tensor = lax.axis_index("seq"), lax.axis_index("tensor")
    return [(seq, (tensor + step) % 8) for step in range(1, 8)]


def attend_kernel(
    blocks, mine, normed, query_hbm, cosine, sine, first, out_hbm, own_stream,
    hidden, key_pages, value_pages,
    kv, parts, landed, queries, peak, total, weighted, query_weight, out_weight,
    send_sems, recv_sems, local_sems,
):
    z, x, core, y, low = place()
    near = lambda step: device(z + step, x, core, y, low)
    far = lambda step: device(z, x + step, core, y, low)
    mate = device(z, x, 1 - core, y, low)
    peers = tensor_peers()
    greet([near(1), near(-1), far(1), far(-1), mate] + peers)
    wires = Wires(send_sems, recv_sems)
    rows = normed.shape[0]
    page_rows = rows // PAGE
    span_size = query_weight.shape[1]
    heads = span_size // HEAD_DIM

    def wrap(v):
        return (v + RING) % RING

    loads = [
        pltpu.make_async_copy(source, target, local_sems.at[number])
        for number, (source, target) in enumerate(
            ((mine, kv.at[core, x, z]), (query_hbm, query_weight), (out_hbm, out_weight))
        )
    ]
    for load in loads:
        load.start()

    mates = []

    def share(z_at, x_at):
        piece = kv.at[core, x_at, z_at]
        mates.append(wires.push(piece, piece, mate))

    def across(z_at):
        piece = kv.at[core, x, z_at]
        ahead = wires.push(piece, piece, far(1))
        back = wires.push(piece, piece, far(-1))
        share(z_at, x)
        return ahead, back

    half = page_rows // 2
    own = kv.at[core, x, z]
    ahead = wires.push(mine, own, near(1))
    back = wires.push(mine, own, near(-1))
    origins = [z, wrap(z - 1), wrap(z + 1), wrap(z + 2)]
    pairs = [(wires.push(mine, own, far(1)), wires.push(mine, own, far(-1)))]
    mates.append(wires.push(mine, own, mate))
    for load in loads:
        load.wait()

    product = jnp.dot(normed[...], query_weight[...], preferred_element_type=jnp.float32)
    for head in range(heads):
        one = product[:, head * HEAD_DIM : (head + 1) * HEAD_DIM]
        one = one * cosine[...] + pltpu.roll(one, HEAD_DIM // 2, 1) * sine[...]
        queries[head] = one.astype(jnp.bfloat16)
    peak[...] = jnp.full(peak.shape, -1e30, jnp.float32)
    total[...] = jnp.zeros(total.shape, jnp.float32)
    weighted[...] = jnp.zeros(weighted.shape, jnp.float32)

    ahead.wait_recv()
    piece = kv.at[core, x, origins[1], pl.ds(0, half)]
    ahead = wires.push(piece, piece, near(1))
    pairs.append(across(origins[1]))
    back.wait_recv()
    piece = kv.at[core, x, origins[2], pl.ds(half, half)]
    back = wires.push(piece, piece, near(-1))
    pairs.append(across(origins[2]))
    ahead.wait_recv()
    back.wait_recv()
    pairs.append(across(origins[3]))
    relays = []

    def onward(number):
        ahead, back = pairs[number]
        ahead.wait_recv()
        if number < 2:
            piece = kv.at[core, wrap(x - 1), origins[number]]
            relays.append(wires.push(piece, piece, far(1)))
        share(origins[number], wrap(x - 1))
        back.wait_recv()
        if number >= 2:
            piece = kv.at[core, wrap(x + 1), origins[number]]
            relays.append(wires.push(piece, piece, far(-1)))
        share(origins[number], wrap(x + 1))

    start_at = first[...]
    here = lax.axis_index("seq") * rows + lax.broadcasted_iota(jnp.int32, (rows, 1), 0)
    keys_in = RING * rows

    def attend(side, x_at):
        line = kv[side, x_at].reshape(keys_in, 2 * span_size)
        column = lax.broadcasted_iota(jnp.int32, (1, keys_in), 1)
        at = ((column // rows * RING + x_at) * 2 + side) * rows + column % rows
        allowed = (at >= start_at) & (at <= here)
        for head in range(heads):
            keys = line[:, head * HEAD_DIM : (head + 1) * HEAD_DIM]
            values = line[:, span_size + head * HEAD_DIM : span_size + (head + 1) * HEAD_DIM]
            scores = lax.dot_general(
                queries[head], keys, (((1,), (1,)), ((), ())), preferred_element_type=jnp.float32
            ) * (HEAD_DIM ** (-0.5))
            old = peak[head]
            new = jnp.maximum(
                old, jnp.max(jnp.where(allowed, scores, -1e30), axis=1, keepdims=True)
            )
            raised = jnp.where(allowed, jnp.exp(scores - new[:, :1]), 0.0)
            keep = jnp.exp(old - new)
            total[head] = total[head] * keep + jnp.sum(raised, axis=1, keepdims=True)
            weighted[head] = weighted[head] * keep + jnp.dot(
                raised.astype(jnp.bfloat16), values, preferred_element_type=jnp.float32
            )
            peak[head] = new

    def arrived(numbers):
        for number in numbers:
            mates[number].wait_recv()

    onward(0)
    attend(core, x)
    onward(1)
    arrived((0, 1, 2, 3))
    attend(1 - core, x)
    onward(2)
    onward(3)
    attend(core, wrap(x - 1))
    attend(core, wrap(x + 1))
    relays[0].wait_recv()
    share(origins[0], wrap(x + 2))
    relays[1].wait_recv()
    share(origins[1], wrap(x + 2))
    arrived((4, 6, 8, 10))
    attend(1 - core, wrap(x - 1))
    relays[2].wait_recv()
    share(origins[2], wrap(x + 2))
    relays[3].wait_recv()
    share(origins[3], wrap(x + 2))
    arrived((5, 7, 9, 11))
    attend(1 - core, wrap(x + 1))
    attend(core, wrap(x + 2))
    arrived((12, 13, 14, 15))
    attend(1 - core, wrap(x + 2))

    attended = jnp.concatenate(
        [(weighted[head] / total[head]).astype(jnp.bfloat16) for head in range(heads)], axis=1
    )
    product = jnp.dot(attended, out_weight[...], preferred_element_type=jnp.float32)
    parts[...] = product.astype(jnp.bfloat16).reshape(parts.shape)
    sums = [
        wires.push(parts.at[peer[1]], landed.at[number], peer) for number, peer in enumerate(peers)
    ]

    for j in range(key_pages.shape[0]):
        block = blocks[j]
        shard = block // page_rows
        page = kv[shard % 2, (shard // 2) % RING, shard // (2 * RING), block % page_rows]
        key_pages[j] = page[:, :span_size]
        value_pages[j] = page[:, span_size:]

    result = own_stream[...] + parts[lax.axis_index("tensor")].astype(jnp.float32)
    for number, copy in enumerate(sums):
        copy.wait_recv()
        result = result + landed[number].astype(jnp.float32)
    hidden[...] = result
    wires.drain()


def attention(blocks, mine, normed, query_weight, cosine, sine, first, out_weight, own_stream):
    rows, columns = mine.shape
    own_rows, features = own_stream.shape
    heads = columns // (2 * HEAD_DIM)
    page_rows = rows // PAGE
    copies = 4 + 8 + 4 + 16 + 7
    inside = pl.BlockSpec(memory_space=pltpu.VMEM)
    anywhere = pl.BlockSpec(memory_space=pl.ANY)
    pages = jax.ShapeDtypeStruct((page_rows, PAGE, columns // 2), mine.dtype)
    state = pltpu.VMEM((heads, rows, HEAD_DIM), jnp.float32)
    return pl.pallas_call(
        attend_kernel,
        out_shape=(jax.ShapeDtypeStruct((own_rows, features), jnp.float32), pages, pages),
        in_specs=[
            pl.BlockSpec(memory_space=pltpu.SMEM),
            inside, inside, anywhere, inside, inside, inside, anywhere, inside,
        ],
        out_specs=(inside, inside, inside),
        scratch_shapes=[
            pltpu.VMEM((2, RING, RING, page_rows, PAGE, columns), mine.dtype),
            pltpu.VMEM((8, own_rows, features), mine.dtype),
            pltpu.VMEM((7, own_rows, features), mine.dtype),
            pltpu.VMEM((heads, rows, HEAD_DIM), mine.dtype),
            state,
            state,
            state,
            pltpu.VMEM(query_weight.shape, query_weight.dtype),
            pltpu.VMEM(out_weight.shape, out_weight.dtype),
            pltpu.SemaphoreType.DMA((copies,)),
            pltpu.SemaphoreType.DMA((copies,)),
            pltpu.SemaphoreType.DMA((3,)),
        ],
        compiler_params=pltpu.CompilerParams(
            collective_id=0, has_side_effects=True, vmem_limit_bytes=62 * 1024 * 1024
        ),
        name="attention",
    )(
        blocks, mine.reshape(page_rows, PAGE, columns), normed, query_weight, cosine, sine, first,
        out_weight, own_stream,
    )

def mixture_kernel(
    mine, hidden, gate, up_part, down, out, rows_all, held, outbox, pair, near_relay, near_land,
    far_relay, far_land, up_relay, up_land, twin_land, final, weight_in, weight_out,
    send_sems, recv_sems, local_sems,
):
    z, x, core, y, low = place()
    up = lambda step: device(z + step, x, core, y, low)
    twin = device(z, x, core, y, 1 - low)
    near = lambda step: device(z, x + step * (1 - core), core, y + step * core, low)
    far = lambda step: device(z, x + step * core, core, y + step * (1 - core), low)
    mate = device(z, x, 1 - core, y, low)
    a, b = x * (1 - core) + y * core, y * (1 - core) + x * core
    peers = tensor_peers()
    ring_y = [near(1), near(-1), far(1), far(-1)]
    greet([up(1), up(-1), mate] + ring_y + peers)
    wires = Wires(send_sems, recv_sems)
    features, width = down.shape[2], gate.shape[2]
    experts_here = gate.shape[0]
    rows = mine.shape[0]

    span = lambda member: pl.ds(pl.multiple_of(member * rows, rows), rows)
    place_own = rows_all.at[core, b, a, z, span(low)]
    loads = [pltpu.make_async_copy(mine, place_own, local_sems.at[0])]
    for number in range(experts_here):
        for kind, source in enumerate((gate, up_part)):
            column = (kind * experts_here + number) * width
            loads.append(
                pltpu.make_async_copy(
                    source.at[number],
                    weight_in.at[:, pl.ds(column, width)],
                    local_sems.at[len(loads)],
                )
            )
        loads.append(
            pltpu.make_async_copy(
                down.at[number],
                weight_out.at[pl.ds(number * width, width)],
                local_sems.at[len(loads)],
            )
        )
    for load in loads:
        load.start()

    def wrap(v):
        return (v + RING) % RING

    def view(side, a_at, b_at, first=0, count=RING):
        return rows_all.at[side, b_at, a_at, pl.ds(first, count)]

    copy = wires.push(mine, place_own, twin)
    loads[0].wait()
    copy.wait_recv()
    starts = [[], [], [], []]

    def launch(z_at):
        piece = rows_all.at[core, b, a, z_at]
        for bundle, peer in zip(starts, (near(1), near(-1), far(1), far(-1))):
            bundle.append(wires.push(piece, piece, peer))

    def wait_all(bundle):
        for copy in bundle:
            copy.wait_recv()

    both = rows_all.at[core, b, a, z]
    ahead = wires.push(both, both, up(1))
    back = wires.push(both, both, up(-1))
    launch(z)
    ahead.wait_recv()
    piece = rows_all.at[core, b, a, wrap(z - 1), pl.ds(0, rows)]
    ahead = wires.push(piece, piece, up(1))
    launch(wrap(z - 1))
    back.wait_recv()
    piece = rows_all.at[core, b, a, wrap(z + 1), pl.ds(rows, rows)]
    back = wires.push(piece, piece, up(-1))
    launch(wrap(z + 1))
    ahead.wait_recv()
    back.wait_recv()
    launch(wrap(z + 2))

    mates = []

    def share(a_at, b_at):
        piece = view(core, a_at, b_at)
        mates.append(wires.push(piece, piece, mate))

    def across(a_at):
        piece = view(core, a_at, b)
        ahead = wires.push(piece, piece, far(1))
        back = wires.push(piece, piece, far(-1))
        share(a_at, b)
        return [ahead], [back]

    origins = [a, wrap(a - 1), wrap(a + 1), wrap(a + 2)]
    share(a, b)
    pairs = [(starts[2], starts[3])]
    wait_all(starts[0])
    piece = view(core, origins[1], b, 0, 2)
    ahead = wires.push(piece, piece, near(1))
    pairs.append(across(origins[1]))
    wait_all(starts[1])
    piece = view(core, origins[2], b, 2, 2)
    back = wires.push(piece, piece, near(-1))
    pairs.append(across(origins[2]))
    ahead.wait_recv()
    back.wait_recv()
    pairs.append(across(origins[3]))

    relays = []

    def onward(number):
        ahead, back = pairs[number]
        wait_all(ahead)
        if number < 2:
            piece = view(core, origins[number], wrap(b - 1))
            relays.append(wires.push(piece, piece, far(1)))
        share(origins[number], wrap(b - 1))
        wait_all(back)
        if number >= 2:
            piece = view(core, origins[number], wrap(b + 1))
            relays.append(wires.push(piece, piece, far(-1)))
        share(origins[number], wrap(b + 1))

    lines = (0, 3, 1, 2)
    first_expert = lax.axis_index("seq") * experts_here
    inner = experts_here * width

    def experts(side, line, target):
        b_at = (y * (1 - side) + x * side + lines[line]) % RING

        @pl.loop(0, RING // BATCH)
        def _(i):
            block = rows_all[side, b_at, pl.ds(i * BATCH, BATCH)]
            block = block.reshape(BATCH * RING * 2 * rows, block.shape[-1])
            product = jnp.dot(
                block[:, :features], weight_in[...], preferred_element_type=jnp.float32
            )
            shares = block[:, features:].astype(jnp.float32)
            names = lax.broadcasted_iota(jnp.int32, shares.shape, 1) % (shares.shape[1] // 2)
            scales = [
                jnp.broadcast_to(
                    jnp.sum(
                        jnp.where(names == first_expert + number, shares, 0.0),
                        axis=1,
                        keepdims=True,
                    ),
                    (shares.shape[0], width),
                )
                for number in range(experts_here)
            ]
            gated = product[:, :inner]
            active = gated / (1.0 + jnp.exp(-gated)) * product[:, inner:]
            active = (active * jnp.concatenate(scales, axis=1)).astype(jnp.bfloat16)
            term = jnp.dot(active, weight_out[...], preferred_element_type=jnp.float32)
            target[line, pl.ds(i * BATCH, BATCH)] = term.astype(jnp.bfloat16).reshape(
                BATCH, RING, 2 * rows, features
            )

    exchanges = {}

    def swap(line):
        for step in (2, 1, 3, 0):
            at = wrap(b + step)
            exchanges[line, step] = wires.push(outbox.at[line, at], pair.at[line, at], mate)

    def ours(line):
        experts(core, line, held)

    def theirs(line, numbers):
        for number in numbers:
            mates[number].wait_recv()
        experts(1 - core, line, outbox)
        swap(line)

    def add(target, first, count, sources):
        @pl.loop(0, count)
        def _(n):
            total = target[first + n].astype(jnp.float32)
            for source in sources:
                total = total + source[n].astype(jnp.float32)
            target[first + n] = total.astype(jnp.bfloat16)

    turns = {}
    lands = {}

    def opening(line):
        at = wrap(a + 2)
        exchanges[line, 2].wait_recv()
        add(held.at[line, at], 0, RING, [pair.at[line, at]])
        turns[line] = (
            wires.push(held.at[line, at, pl.ds(0, 2)], near_relay.at[line, 0], near(1)),
            wires.push(held.at[line, at, pl.ds(2, 2)], near_relay.at[line, 1], near(-1)),
        )

    def middle(line):
        for side, step in ((0, 1), (1, 3)):
            at = wrap(a + step)
            exchanges[line, step].wait_recv()
            piece, other = held.at[line, at], pair.at[line, at]
            add(piece, 2 - 2 * side, 2, [other.at[pl.ds(2 - 2 * side, 2)]])
            turns[line][side].wait_recv()
            add(piece, 2 * side, 2, [other.at[pl.ds(2 * side, 2)], near_relay.at[line, side]])
            lands[line, side] = wires.push(piece, near_land.at[line, side], near(1 - 2 * side))

    def closing(line):
        exchanges[line, 0].wait_recv()
        lands[line, 0].wait_recv()
        lands[line, 1].wait_recv()
        add(held.at[line, a], 0, RING, [pair.at[line, a], near_land.at[line, 0], near_land.at[line, 1]])

    def relayed(number):
        relays[number].wait_recv()
        share(origins[number], wrap(b + 2))

    onward(0)
    for load in loads[1:]:
        load.wait()
    ours(0)
    onward(1)
    theirs(0, (0, 1, 2, 3))
    onward(2)
    onward(3)
    opening(0)
    ours(1)
    relayed(0)
    relayed(1)
    theirs(1, (4, 6, 8, 10))
    ours(2)
    relayed(2)
    relayed(3)
    opening(1)
    middle(0)
    theirs(3, (12, 13, 14, 15))
    ours(3)
    opening(3)
    theirs(2, (5, 7, 9, 11))
    opening(2)
    middle(1)
    middle(3)
    middle(2)
    closing(3)

    line_sum = lambda line: held.at[line, a]
    far_turns = (
        wires.push(held.at[3, a, pl.ds(0, 2)], far_relay.at[0], far(1)),
        wires.push(held.at[3, a, pl.ds(2, 2)], far_relay.at[1], far(-1)),
    )
    closing(2)
    closing(1)
    closing(0)
    for side, line in ((0, 2), (1, 1)):
        far_turns[side].wait_recv()
        add(line_sum(line), 2 * side, 2, [far_relay.at[side]])
    far_lands = {}
    for step in (2, 1, 3, 0):
        at = wrap(z + step)
        far_lands[step] = [
            wires.push(line_sum(line).at[at], far_land.at[side, at], far(1 - 2 * side))
            for side, line in ((0, 2), (1, 1))
        ]
    last = line_sum(0)

    def finish(step):
        at = wrap(z + step)
        wait_all(far_lands[step])
        add(last, at, 1, [far_land.at[0, pl.ds(at, 1)], far_land.at[1, pl.ds(at, 1)]])

    finish(2)
    beyond = wrap(z + 2)
    up_turns = [
        wires.push(last.at[beyond, pl.ds(side * rows, rows)], up_relay.at[side], up(step))
        for side, step in ((0, 1), (1, -1))
    ]
    up_lands = []
    for side, step in ((0, 1), (1, 3)):
        finish(step)
        up_turns[side].wait_recv()
        beside = wrap(z + step)
        part = pl.ds(side * rows, rows)
        total = last[beside, part].astype(jnp.float32) + up_relay[side].astype(jnp.float32)
        last[beside, part] = total.astype(jnp.bfloat16)
        up_lands.append(wires.push(last.at[beside], up_land.at[side], up(1 - 2 * side)))
    finish(0)
    for copy in up_lands:
        copy.wait_recv()
    total = last[z].astype(jnp.float32)
    total = total + up_land[0].astype(jnp.float32) + up_land[1].astype(jnp.float32)
    last[z] = total.astype(jnp.bfloat16)
    copy = wires.push(last.at[z, span(1 - low)], twin_land, twin)
    copy.wait_recv()
    total = hidden[...] + last[z, span(low)].astype(jnp.float32)
    final[...] = (total + twin_land[...].astype(jnp.float32)).astype(jnp.bfloat16)

    local = pltpu.make_async_copy(final, out.at[y * 2 + low], local_sems.at[0])
    local.start()
    results = [wires.push(final, out.at[y * 2 + low], peer) for peer in peers]
    local.wait()
    for copy in results:
        copy.wait_recv()
    wires.drain()


def mixture(mine, hidden, gate_weight, up_weight, down_weight):
    rows, columns = mine.shape
    features = hidden.shape[1]
    here, _, width = gate_weight.shape
    two = 2 * rows
    kind = mine.dtype
    copies = 1 + 4 + 16 + 2 + 6 + 4 + 16 + 16 + 16 + 10 + 4 + 1 + 7
    grain = (RING, two, features)
    halves = (2, two, features)
    scratch = lambda *shape: pltpu.VMEM(shape, kind)
    anywhere = pl.BlockSpec(memory_space=pl.ANY)
    inside = pl.BlockSpec(memory_space=pltpu.VMEM)
    return pl.pallas_call(
        mixture_kernel,
        out_shape=jax.ShapeDtypeStruct((8, rows, features), kind),
        in_specs=[inside, inside, anywhere, anywhere, anywhere],
        out_specs=anywhere,
        scratch_shapes=[
            scratch(2, RING, RING, RING, two, columns),
            scratch(RING, RING, *grain),
            scratch(RING, RING, *grain),
            scratch(RING, RING, *grain),
            scratch(RING, 2, *halves),
            scratch(RING, 2, *grain),
            scratch(2, *halves),
            scratch(2, *grain),
            scratch(2, rows, features),
            scratch(2, two, features),
            scratch(rows, features),
            scratch(rows, features),
            scratch(features, 2 * here * width),
            scratch(here * width, features),
            pltpu.SemaphoreType.DMA((copies,)),
            pltpu.SemaphoreType.DMA((copies,)),
            pltpu.SemaphoreType.DMA((1 + 3 * here,)),
        ],
        compiler_params=pltpu.CompilerParams(
            collective_id=1, has_side_effects=True, vmem_limit_bytes=62 * 1024 * 1024
        ),
        name="mixture",
    )(mine, hidden, gate_weight, up_weight, down_weight).reshape(8 * rows, features)


def rms_scale(matrix, scaling):
    mean_square = jnp.mean(matrix * matrix, axis=-1, keepdims=True)
    return matrix * lax.rsqrt(mean_square + epsilon) * scaling


def segment_info(lengths, places):
    starts = jnp.cumsum(lengths) - lengths
    inside = (places[:, None] >= starts[None, :]).astype(jnp.int32)
    segment = jnp.sum(inside, axis=1) - 1
    slot_ids = jnp.arange(starts.shape[0], dtype=jnp.int32)
    seg_start = jnp.sum(
        jnp.where(slot_ids[None, :] == segment[:, None], starts[None, :], 0), axis=1
    )
    return (segment, places - seg_start)


def rotate(matrix, position):
    half_dim = matrix.shape[-1] // 2
    frequency = jnp.exp(
        -jnp.log(rope_base) * jnp.arange(half_dim, dtype=jnp.float32) * (2.0 / matrix.shape[-1])
    )
    angles = position.astype(jnp.float32)[:, None] * frequency[None, :]
    cosine = jnp.cos(angles)[:, None, :]
    sine_part = jnp.sin(angles)[:, None, :]
    first_half = matrix[..., :half_dim]
    second = matrix[..., half_dim:]
    return jnp.concatenate(
        [first_half * cosine - second * sine_part, second * cosine + first_half * sine_part],
        axis=-1,
    )


def local(
    tokens,
    lengths,
    page_table,
    attention_gain,
    query_weight,
    key_weight,
    value_weight,
    out_weight,
    expert_gain,
    router_weight,
    expert_ids,
    gate_weight,
    up_weight,
    down_weight,
):
    row_count = tokens.shape[0]
    feature_count = tokens.shape[1]
    span_size = query_weight.shape[1]
    head_count = span_size // HEAD_DIM
    shard_id = lax.axis_index("seq")
    places = shard_id * row_count + jnp.arange(row_count, dtype=jnp.int32)
    segment, position = segment_info(lengths, places)
    stream = tokens.astype(jnp.float32)
    normed = rms_scale(stream, attention_gain).astype(jnp.bfloat16)

    def project(weight):
        return jnp.dot(normed, weight, preferred_element_type=jnp.float32)

    def turned(matrix):
        return rotate(matrix.reshape(row_count, head_count, HEAD_DIM), position).astype(
            jnp.bfloat16
        )

    key_rows = turned(project(key_weight)).reshape(row_count, span_size)
    value_rows = project(value_weight).astype(jnp.bfloat16)
    half_dim = HEAD_DIM // 2
    frequency = jnp.exp(
        -jnp.log(rope_base) * jnp.arange(half_dim, dtype=jnp.float32) * (2.0 / HEAD_DIM)
    )
    angles = position.astype(jnp.float32)[:, None] * frequency[None, :]
    cosine = jnp.concatenate([jnp.cos(angles), jnp.cos(angles)], axis=1)
    sine = jnp.concatenate([-jnp.sin(angles), jnp.sin(angles)], axis=1)

    page_rows = row_count // PAGE
    my_pages = shard_id * page_rows + jnp.arange(page_rows, dtype=jnp.int32)
    block_ids = jnp.arange(page_table.shape[0], dtype=jnp.int32)
    blocks = jnp.sum(
        jnp.where(page_table[None, :] == my_pages[:, None], block_ids[None, :], 0), axis=1
    )

    member = lax.axis_index("tensor")
    own_rows = row_count // lax.axis_size("tensor")
    own_stream = lax.dynamic_slice_in_dim(tokens, member * own_rows, own_rows, 0)
    own_ids = lax.dynamic_slice_in_dim(expert_ids, member * own_rows, own_rows, 0)
    hidden, key_cache, value_cache = attention(
        blocks,
        jnp.concatenate([key_rows, value_rows], axis=1),
        normed,
        query_weight,
        cosine,
        sine,
        (places - position)[:, None],
        out_weight,
        own_stream.astype(jnp.float32),
    )
    moe_input = rms_scale(hidden, expert_gain).astype(jnp.bfloat16)
    expert_count = router_weight.shape[1]
    probability = jax.nn.softmax(
        jnp.dot(moe_input, router_weight, preferred_element_type=jnp.float32), axis=-1
    )
    expert_range = jnp.arange(expert_count, dtype=jnp.int32)
    named = jnp.any(own_ids[:, :, None] == expert_range[None, None, :], axis=1)
    share = jnp.where(named, probability, 0.0)
    share_high = share.astype(jnp.bfloat16)
    share_low = (share - share_high.astype(jnp.float32)).astype(jnp.bfloat16)

    mine = jnp.concatenate([moe_input, share_high, share_low], axis=1)
    layer_out = mixture(mine, hidden, gate_weight, up_weight, down_weight)
    return (layer_out, key_cache, value_cache)


def solution(mesh):
    return jax.shard_map(
        local,
        mesh=mesh,
        in_specs=(
            P("seq", None),
            P(),
            P(),
            P(),
            P(None, "tensor"),
            P(None, "tensor"),
            P(None, "tensor"),
            P("tensor", None),
            P(),
            P(),
            P("seq", None),
            P("seq", None, "tensor"),
            P("seq", None, "tensor"),
            P("seq", "tensor", None),
        ),
        out_specs=(P("seq", None), P("seq", None, "tensor"), P("seq", None, "tensor")),
        check_vma=False,
    )
```

```python
import functools

import jax
import jax.numpy as jnp
from jax import lax
from jax.experimental import pallas as pl
from jax.experimental.pallas import tpu as pltpu
from jax.sharding import PartitionSpec as P

HEAD_DIM = 128
PAGE = 16
RING = 4
BATCH = 2
MESH = pl.DeviceIdType.MESH

epsilon = 1e-05
rope_base = 10000.0


def place():
    seq = lax.axis_index("seq")
    tensor = lax.axis_index("tensor")
    return seq // 8, (seq // 2) % RING, seq % 2, tensor // 2, tensor % 2


def device(z, x, core, y, low):
    z, x, y = (z + RING) % RING, (x + RING) % RING, (y + RING) % RING
    return ((z * RING + x) * 2 + core, y * 2 + low)


def greet(peers):
    barrier = pltpu.get_barrier_semaphore()
    for peer in peers:
        pl.semaphore_signal(barrier, inc=1, device_id=peer, device_id_type=MESH)
    pl.semaphore_wait(barrier, len(peers))


class Wires:
    def __init__(self, send_sems, recv_sems):
        self.send_sems, self.recv_sems, self.copies = send_sems, recv_sems, []

    def push(self, source, target, peer):
        number = len(self.copies)
        copy = pltpu.make_async_remote_copy(
            src_ref=source,
            dst_ref=target,
            send_sem=self.send_sems.at[number],
            recv_sem=self.recv_sems.at[number],
            device_id=peer,
            device_id_type=MESH,
        )
        copy.start()
        self.copies.append(copy)
        return copy

    def drain(self):
        for copy in self.copies:
            copy.wait_send()


def tensor_peers():
    seq, tensor = lax.axis_index("seq"), lax.axis_index("tensor")
    return [(seq, (tensor + step) % 8) for step in range(1, 8)]


def attend_kernel(
    blocks, mine, normed, query_weight, cosine, sine, first, out_weight, own_stream,
    hidden, key_pages, value_pages,
    kv, parts, landed, queries, peak, total, weighted,
    send_sems, recv_sems, local_sem,
):
    z, x, core, y, low = place()
    near = lambda step: device(z + step, x, core, y, low)
    far = lambda step: device(z, x + step, core, y, low)
    mate = device(z, x, 1 - core, y, low)
    peers = tensor_peers()
    greet([near(1), near(-1), far(1), far(-1), mate] + peers)
    wires = Wires(send_sems, recv_sems)
    rows = normed.shape[0]
    page_rows = rows // PAGE
    span_size = query_weight.shape[1]
    heads = span_size // HEAD_DIM

    def wrap(v):
        return (v + RING) % RING

    local = pltpu.make_async_copy(mine, kv.at[core, x, z], local_sem)
    local.start()
    local.wait()

    mates = []

    def share(z_at, x_at):
        piece = kv.at[core, x_at, z_at]
        mates.append(wires.push(piece, piece, mate))

    def across(z_at):
        piece = kv.at[core, x, z_at]
        ahead = wires.push(piece, piece, far(1))
        back = wires.push(piece, piece, far(-1))
        share(z_at, x)
        return ahead, back

    half = page_rows // 2
    own = kv.at[core, x, z]
    ahead = wires.push(own, own, near(1))
    back = wires.push(own, own, near(-1))
    origins = [z, wrap(z - 1), wrap(z + 1), wrap(z + 2)]
    pairs = [across(origins[0])]

    product = jnp.dot(normed[...], query_weight[...], preferred_element_type=jnp.float32)
    for head in range(heads):
        one = product[:, head * HEAD_DIM : (head + 1) * HEAD_DIM]
        one = one * cosine[...] + pltpu.roll(one, HEAD_DIM // 2, 1) * sine[...]
        queries[head] = one.astype(jnp.bfloat16)
    peak[...] = jnp.full(peak.shape, -1e30, jnp.float32)
    total[...] = jnp.zeros(total.shape, jnp.float32)
    weighted[...] = jnp.zeros(weighted.shape, jnp.float32)

    ahead.wait_recv()
    piece = kv.at[core, x, origins[1], pl.ds(0, half)]
    ahead = wires.push(piece, piece, near(1))
    pairs.append(across(origins[1]))
    back.wait_recv()
    piece = kv.at[core, x, origins[2], pl.ds(half, half)]
    back = wires.push(piece, piece, near(-1))
    pairs.append(across(origins[2]))
    ahead.wait_recv()
    back.wait_recv()
    pairs.append(across(origins[3]))
    relays = []

    def onward(number):
        ahead, back = pairs[number]
        ahead.wait_recv()
        if number < 2:
            piece = kv.at[core, wrap(x - 1), origins[number]]
            relays.append(wires.push(piece, piece, far(1)))
        share(origins[number], wrap(x - 1))
        back.wait_recv()
        if number >= 2:
            piece = kv.at[core, wrap(x + 1), origins[number]]
            relays.append(wires.push(piece, piece, far(-1)))
        share(origins[number], wrap(x + 1))

    start_at = first[...]
    here = lax.axis_index("seq") * rows + lax.broadcasted_iota(jnp.int32, (rows, 1), 0)
    keys_in = RING * rows

    def attend(side, x_at):
        line = kv[side, x_at].reshape(keys_in, 2 * span_size)
        column = lax.broadcasted_iota(jnp.int32, (1, keys_in), 1)
        at = ((column // rows * RING + x_at) * 2 + side) * rows + column % rows
        allowed = (at >= start_at) & (at <= here)
        for head in range(heads):
            keys = line[:, head * HEAD_DIM : (head + 1) * HEAD_DIM]
            values = line[:, span_size + head * HEAD_DIM : span_size + (head + 1) * HEAD_DIM]
            scores = lax.dot_general(
                queries[head], keys, (((1,), (1,)), ((), ())), preferred_element_type=jnp.float32
            ) * (HEAD_DIM ** (-0.5))
            old = peak[head]
            new = jnp.maximum(
                old, jnp.max(jnp.where(allowed, scores, -1e30), axis=1, keepdims=True)
            )
            raised = jnp.where(allowed, jnp.exp(scores - new[:, :1]), 0.0)
            keep = jnp.exp(old - new)
            total[head] = total[head] * keep + jnp.sum(raised, axis=1, keepdims=True)
            weighted[head] = weighted[head] * keep + jnp.dot(
                raised.astype(jnp.bfloat16), values, preferred_element_type=jnp.float32
            )
            peak[head] = new

    def arrived(numbers):
        for number in numbers:
            mates[number].wait_recv()

    onward(0)
    attend(core, x)
    onward(1)
    arrived((0, 1, 2, 3))
    attend(1 - core, x)
    onward(2)
    onward(3)
    attend(core, wrap(x - 1))
    attend(core, wrap(x + 1))
    relays[0].wait_recv()
    share(origins[0], wrap(x + 2))
    relays[1].wait_recv()
    share(origins[1], wrap(x + 2))
    arrived((4, 6, 8, 10))
    attend(1 - core, wrap(x - 1))
    relays[2].wait_recv()
    share(origins[2], wrap(x + 2))
    relays[3].wait_recv()
    share(origins[3], wrap(x + 2))
    arrived((5, 7, 9, 11))
    attend(1 - core, wrap(x + 1))
    attend(core, wrap(x + 2))
    arrived((12, 13, 14, 15))
    attend(1 - core, wrap(x + 2))

    attended = jnp.concatenate(
        [(weighted[head] / total[head]).astype(jnp.bfloat16) for head in range(heads)], axis=1
    )
    product = jnp.dot(attended, out_weight[...], preferred_element_type=jnp.float32)
    parts[...] = product.astype(jnp.bfloat16).reshape(parts.shape)
    sums = [
        wires.push(parts.at[peer[1]], landed.at[number], peer) for number, peer in enumerate(peers)
    ]

    for j in range(key_pages.shape[0]):
        block = blocks[j]
        shard = block // page_rows
        page = kv[shard % 2, (shard // 2) % RING, shard // (2 * RING), block % page_rows]
        key_pages[j] = page[:, :span_size]
        value_pages[j] = page[:, span_size:]

    result = own_stream[...] + parts[lax.axis_index("tensor")].astype(jnp.float32)
    for number, copy in enumerate(sums):
        copy.wait_recv()
        result = result + landed[number].astype(jnp.float32)
    hidden[...] = result
    wires.drain()


def attention(blocks, mine, normed, query_weight, cosine, sine, first, out_weight, own_stream):
    rows, columns = mine.shape
    own_rows, features = own_stream.shape
    heads = columns // (2 * HEAD_DIM)
    page_rows = rows // PAGE
    copies = 4 + 8 + 4 + 16 + 7
    inside = pl.BlockSpec(memory_space=pltpu.VMEM)
    pages = jax.ShapeDtypeStruct((page_rows, PAGE, columns // 2), mine.dtype)
    state = pltpu.VMEM((heads, rows, HEAD_DIM), jnp.float32)
    return pl.pallas_call(
        attend_kernel,
        out_shape=(jax.ShapeDtypeStruct((own_rows, features), jnp.float32), pages, pages),
        in_specs=[pl.BlockSpec(memory_space=pltpu.SMEM)] + [inside] * 8,
        out_specs=(inside, inside, inside),
        scratch_shapes=[
            pltpu.VMEM((2, RING, RING, page_rows, PAGE, columns), mine.dtype),
            pltpu.VMEM((8, own_rows, features), mine.dtype),
            pltpu.VMEM((7, own_rows, features), mine.dtype),
            pltpu.VMEM((heads, rows, HEAD_DIM), mine.dtype),
            state,
            state,
            state,
            pltpu.SemaphoreType.DMA((copies,)),
            pltpu.SemaphoreType.DMA((copies,)),
            pltpu.SemaphoreType.DMA,
        ],
        compiler_params=pltpu.CompilerParams(
            collective_id=0, has_side_effects=True, vmem_limit_bytes=40 * 1024 * 1024
        ),
        name="attention",
    )(
        blocks, mine.reshape(page_rows, PAGE, columns), normed, query_weight, cosine, sine, first,
        out_weight, own_stream,
    )

def mixture_kernel(
    mine, hidden, gate, up_part, down, out, rows_all, held, outbox, pair, near_relay, near_land,
    far_relay, far_land, up_relay, up_land, twin_land, final, weight_in, weight_out,
    send_sems, recv_sems, local_sems,
):
    z, x, core, y, low = place()
    up = lambda step: device(z + step, x, core, y, low)
    twin = device(z, x, core, y, 1 - low)
    near = lambda step: device(z, x + step * (1 - core), core, y + step * core, low)
    far = lambda step: device(z, x + step * core, core, y + step * (1 - core), low)
    mate = device(z, x, 1 - core, y, low)
    a, b = x * (1 - core) + y * core, y * (1 - core) + x * core
    peers = tensor_peers()
    ring_y = [near(1), near(-1), far(1), far(-1)]
    greet([up(1), up(-1), mate] + ring_y + peers)
    wires = Wires(send_sems, recv_sems)
    features, width = down.shape[2], gate.shape[2]
    experts_here = gate.shape[0]
    rows = mine.shape[0]

    span = lambda member: pl.ds(pl.multiple_of(member * rows, rows), rows)
    place_own = rows_all.at[core, b, a, z, span(low)]
    loads = [pltpu.make_async_copy(mine, place_own, local_sems.at[0])]
    for number in range(experts_here):
        for kind, source in enumerate((gate, up_part)):
            column = (kind * experts_here + number) * width
            loads.append(
                pltpu.make_async_copy(
                    source.at[number],
                    weight_in.at[:, pl.ds(column, width)],
                    local_sems.at[len(loads)],
                )
            )
        loads.append(
            pltpu.make_async_copy(
                down.at[number],
                weight_out.at[pl.ds(number * width, width)],
                local_sems.at[len(loads)],
            )
        )
    for load in loads:
        load.start()

    def wrap(v):
        return (v + RING) % RING

    def view(side, a_at, b_at, first=0, count=RING):
        return rows_all.at[side, b_at, a_at, pl.ds(first, count)]

    copy = wires.push(mine, place_own, twin)
    loads[0].wait()
    copy.wait_recv()
    starts = [[], [], [], []]

    def launch(z_at):
        piece = rows_all.at[core, b, a, z_at]
        for bundle, peer in zip(starts, (near(1), near(-1), far(1), far(-1))):
            bundle.append(wires.push(piece, piece, peer))

    def wait_all(bundle):
        for copy in bundle:
            copy.wait_recv()

    both = rows_all.at[core, b, a, z]
    ahead = wires.push(both, both, up(1))
    back = wires.push(both, both, up(-1))
    launch(z)
    ahead.wait_recv()
    piece = rows_all.at[core, b, a, wrap(z - 1), pl.ds(0, rows)]
    ahead = wires.push(piece, piece, up(1))
    launch(wrap(z - 1))
    back.wait_recv()
    piece = rows_all.at[core, b, a, wrap(z + 1), pl.ds(rows, rows)]
    back = wires.push(piece, piece, up(-1))
    launch(wrap(z + 1))
    ahead.wait_recv()
    back.wait_recv()
    launch(wrap(z + 2))

    mates = []

    def share(a_at, b_at):
        piece = view(core, a_at, b_at)
        mates.append(wires.push(piece, piece, mate))

    def across(a_at):
        piece = view(core, a_at, b)
        ahead = wires.push(piece, piece, far(1))
        back = wires.push(piece, piece, far(-1))
        share(a_at, b)
        return [ahead], [back]

    origins = [a, wrap(a - 1), wrap(a + 1), wrap(a + 2)]
    share(a, b)
    pairs = [(starts[2], starts[3])]
    wait_all(starts[0])
    piece = view(core, origins[1], b, 0, 2)
    ahead = wires.push(piece, piece, near(1))
    pairs.append(across(origins[1]))
    wait_all(starts[1])
    piece = view(core, origins[2], b, 2, 2)
    back = wires.push(piece, piece, near(-1))
    pairs.append(across(origins[2]))
    ahead.wait_recv()
    back.wait_recv()
    pairs.append(across(origins[3]))

    relays = []

    def onward(number):
        ahead, back = pairs[number]
        wait_all(ahead)
        if number < 2:
            piece = view(core, origins[number], wrap(b - 1))
            relays.append(wires.push(piece, piece, far(1)))
        share(origins[number], wrap(b - 1))
        wait_all(back)
        if number >= 2:
            piece = view(core, origins[number], wrap(b + 1))
            relays.append(wires.push(piece, piece, far(-1)))
        share(origins[number], wrap(b + 1))

    lines = (0, 3, 1, 2)
    first_expert = lax.axis_index("seq") * experts_here
    inner = experts_here * width

    def experts(side, line, target):
        b_at = (y * (1 - side) + x * side + lines[line]) % RING

        @pl.loop(0, RING // BATCH)
        def _(i):
            block = rows_all[side, b_at, pl.ds(i * BATCH, BATCH)]
            block = block.reshape(BATCH * RING * 2 * rows, block.shape[-1])
            product = jnp.dot(
                block[:, :features], weight_in[...], preferred_element_type=jnp.float32
            )
            shares = block[:, features:].astype(jnp.float32)
            names = lax.broadcasted_iota(jnp.int32, shares.shape, 1) % (shares.shape[1] // 2)
            scales = [
                jnp.broadcast_to(
                    jnp.sum(
                        jnp.where(names == first_expert + number, shares, 0.0),
                        axis=1,
                        keepdims=True,
                    ),
                    (shares.shape[0], width),
                )
                for number in range(experts_here)
            ]
            gated = product[:, :inner]
            active = gated / (1.0 + jnp.exp(-gated)) * product[:, inner:]
            active = (active * jnp.concatenate(scales, axis=1)).astype(jnp.bfloat16)
            term = jnp.dot(active, weight_out[...], preferred_element_type=jnp.float32)
            target[line, pl.ds(i * BATCH, BATCH)] = term.astype(jnp.bfloat16).reshape(
                BATCH, RING, 2 * rows, features
            )

    exchanges = {}

    def swap(line):
        for step in (2, 1, 3, 0):
            at = wrap(b + step)
            exchanges[line, step] = wires.push(outbox.at[line, at], pair.at[line, at], mate)

    def ours(line):
        experts(core, line, held)

    def theirs(line, numbers):
        for number in numbers:
            mates[number].wait_recv()
        experts(1 - core, line, outbox)
        swap(line)

    def add(target, first, count, sources):
        @pl.loop(0, count)
        def _(n):
            total = target[first + n].astype(jnp.float32)
            for source in sources:
                total = total + source[n].astype(jnp.float32)
            target[first + n] = total.astype(jnp.bfloat16)

    turns = {}
    lands = {}

    def opening(line):
        at = wrap(a + 2)
        exchanges[line, 2].wait_recv()
        add(held.at[line, at], 0, RING, [pair.at[line, at]])
        turns[line] = (
            wires.push(held.at[line, at, pl.ds(0, 2)], near_relay.at[line, 0], near(1)),
            wires.push(held.at[line, at, pl.ds(2, 2)], near_relay.at[line, 1], near(-1)),
        )

    def middle(line):
        for side, step in ((0, 1), (1, 3)):
            at = wrap(a + step)
            exchanges[line, step].wait_recv()
            piece, other = held.at[line, at], pair.at[line, at]
            add(piece, 2 - 2 * side, 2, [other.at[pl.ds(2 - 2 * side, 2)]])
            turns[line][side].wait_recv()
            add(piece, 2 * side, 2, [other.at[pl.ds(2 * side, 2)], near_relay.at[line, side]])
            lands[line, side] = wires.push(piece, near_land.at[line, side], near(1 - 2 * side))

    def closing(line):
        exchanges[line, 0].wait_recv()
        lands[line, 0].wait_recv()
        lands[line, 1].wait_recv()
        add(held.at[line, a], 0, RING, [pair.at[line, a], near_land.at[line, 0], near_land.at[line, 1]])

    def relayed(number):
        relays[number].wait_recv()
        share(origins[number], wrap(b + 2))

    onward(0)
    for load in loads[1:]:
        load.wait()
    ours(0)
    onward(1)
    theirs(0, (0, 1, 2, 3))
    onward(2)
    onward(3)
    opening(0)
    ours(1)
    relayed(0)
    relayed(1)
    theirs(1, (4, 6, 8, 10))
    ours(2)
    relayed(2)
    relayed(3)
    opening(1)
    middle(0)
    theirs(3, (12, 13, 14, 15))
    ours(3)
    opening(3)
    theirs(2, (5, 7, 9, 11))
    opening(2)
    middle(1)
    middle(3)
    middle(2)
    closing(3)

    line_sum = lambda line: held.at[line, a]
    far_turns = (
        wires.push(held.at[3, a, pl.ds(0, 2)], far_relay.at[0], far(1)),
        wires.push(held.at[3, a, pl.ds(2, 2)], far_relay.at[1], far(-1)),
    )
    closing(2)
    closing(1)
    closing(0)
    for side, line in ((0, 2), (1, 1)):
        far_turns[side].wait_recv()
        add(line_sum(line), 2 * side, 2, [far_relay.at[side]])
    far_lands = {}
    for step in (2, 1, 3, 0):
        at = wrap(z + step)
        far_lands[step] = [
            wires.push(line_sum(line).at[at], far_land.at[side, at], far(1 - 2 * side))
            for side, line in ((0, 2), (1, 1))
        ]
    last = line_sum(0)

    def finish(step):
        at = wrap(z + step)
        wait_all(far_lands[step])
        add(last, at, 1, [far_land.at[0, pl.ds(at, 1)], far_land.at[1, pl.ds(at, 1)]])

    finish(2)
    beyond = wrap(z + 2)
    up_turns = [
        wires.push(last.at[beyond, pl.ds(side * rows, rows)], up_relay.at[side], up(step))
        for side, step in ((0, 1), (1, -1))
    ]
    up_lands = []
    for side, step in ((0, 1), (1, 3)):
        finish(step)
        up_turns[side].wait_recv()
        beside = wrap(z + step)
        part = pl.ds(side * rows, rows)
        total = last[beside, part].astype(jnp.float32) + up_relay[side].astype(jnp.float32)
        last[beside, part] = total.astype(jnp.bfloat16)
        up_lands.append(wires.push(last.at[beside], up_land.at[side], up(1 - 2 * side)))
    finish(0)
    for copy in up_lands:
        copy.wait_recv()
    total = last[z].astype(jnp.float32)
    total = total + up_land[0].astype(jnp.float32) + up_land[1].astype(jnp.float32)
    last[z] = total.astype(jnp.bfloat16)
    copy = wires.push(last.at[z, span(1 - low)], twin_land, twin)
    copy.wait_recv()
    total = hidden[...] + last[z, span(low)].astype(jnp.float32)
    final[...] = (total + twin_land[...].astype(jnp.float32)).astype(jnp.bfloat16)

    local = pltpu.make_async_copy(final, out.at[y * 2 + low], local_sems.at[0])
    local.start()
    results = [wires.push(final, out.at[y * 2 + low], peer) for peer in peers]
    local.wait()
    for copy in results:
        copy.wait_recv()
    wires.drain()


def mixture(mine, hidden, gate_weight, up_weight, down_weight):
    rows, columns = mine.shape
    features = hidden.shape[1]
    here, _, width = gate_weight.shape
    two = 2 * rows
    kind = mine.dtype
    copies = 1 + 4 + 16 + 2 + 6 + 4 + 16 + 16 + 16 + 10 + 4 + 1 + 7
    grain = (RING, two, features)
    halves = (2, two, features)
    scratch = lambda *shape: pltpu.VMEM(shape, kind)
    anywhere = pl.BlockSpec(memory_space=pl.ANY)
    inside = pl.BlockSpec(memory_space=pltpu.VMEM)
    return pl.pallas_call(
        mixture_kernel,
        out_shape=jax.ShapeDtypeStruct((8, rows, features), kind),
        in_specs=[inside, inside, anywhere, anywhere, anywhere],
        out_specs=anywhere,
        scratch_shapes=[
            scratch(2, RING, RING, RING, two, columns),
            scratch(RING, RING, *grain),
            scratch(RING, RING, *grain),
            scratch(RING, RING, *grain),
            scratch(RING, 2, *halves),
            scratch(RING, 2, *grain),
            scratch(2, *halves),
            scratch(2, *grain),
            scratch(2, rows, features),
            scratch(2, two, features),
            scratch(rows, features),
            scratch(rows, features),
            scratch(features, 2 * here * width),
            scratch(here * width, features),
            pltpu.SemaphoreType.DMA((copies,)),
            pltpu.SemaphoreType.DMA((copies,)),
            pltpu.SemaphoreType.DMA((1 + 3 * here,)),
        ],
        compiler_params=pltpu.CompilerParams(
            collective_id=1, has_side_effects=True, vmem_limit_bytes=62 * 1024 * 1024
        ),
        name="mixture",
    )(mine, hidden, gate_weight, up_weight, down_weight).reshape(8 * rows, features)


def rms_scale(matrix, scaling):
    mean_square = jnp.mean(matrix * matrix, axis=-1, keepdims=True)
    return matrix * lax.rsqrt(mean_square + epsilon) * scaling


def segment_info(lengths, places):
    starts = jnp.cumsum(lengths) - lengths
    inside = (places[:, None] >= starts[None, :]).astype(jnp.int32)
    segment = jnp.sum(inside, axis=1) - 1
    slot_ids = jnp.arange(starts.shape[0], dtype=jnp.int32)
    seg_start = jnp.sum(
        jnp.where(slot_ids[None, :] == segment[:, None], starts[None, :], 0), axis=1
    )
    return (segment, places - seg_start)


def rotate(matrix, position):
    half_dim = matrix.shape[-1] // 2
    frequency = jnp.exp(
        -jnp.log(rope_base) * jnp.arange(half_dim, dtype=jnp.float32) * (2.0 / matrix.shape[-1])
    )
    angles = position.astype(jnp.float32)[:, None] * frequency[None, :]
    cosine = jnp.cos(angles)[:, None, :]
    sine_part = jnp.sin(angles)[:, None, :]
    first_half = matrix[..., :half_dim]
    second = matrix[..., half_dim:]
    return jnp.concatenate(
        [first_half * cosine - second * sine_part, second * cosine + first_half * sine_part],
        axis=-1,
    )


def local(
    tokens,
    lengths,
    page_table,
    attention_gain,
    query_weight,
    key_weight,
    value_weight,
    out_weight,
    expert_gain,
    router_weight,
    expert_ids,
    gate_weight,
    up_weight,
    down_weight,
):
    row_count = tokens.shape[0]
    feature_count = tokens.shape[1]
    span_size = query_weight.shape[1]
    head_count = span_size // HEAD_DIM
    shard_id = lax.axis_index("seq")
    places = shard_id * row_count + jnp.arange(row_count, dtype=jnp.int32)
    segment, position = segment_info(lengths, places)
    stream = tokens.astype(jnp.float32)
    normed = rms_scale(stream, attention_gain).astype(jnp.bfloat16)

    def project(weight):
        return jnp.dot(normed, weight, preferred_element_type=jnp.float32)

    def turned(matrix):
        return rotate(matrix.reshape(row_count, head_count, HEAD_DIM), position).astype(
            jnp.bfloat16
        )

    key_rows = turned(project(key_weight)).reshape(row_count, span_size)
    value_rows = project(value_weight).astype(jnp.bfloat16)
    half_dim = HEAD_DIM // 2
    frequency = jnp.exp(
        -jnp.log(rope_base) * jnp.arange(half_dim, dtype=jnp.float32) * (2.0 / HEAD_DIM)
    )
    angles = position.astype(jnp.float32)[:, None] * frequency[None, :]
    cosine = jnp.concatenate([jnp.cos(angles), jnp.cos(angles)], axis=1)
    sine = jnp.concatenate([-jnp.sin(angles), jnp.sin(angles)], axis=1)

    page_rows = row_count // PAGE
    my_pages = shard_id * page_rows + jnp.arange(page_rows, dtype=jnp.int32)
    block_ids = jnp.arange(page_table.shape[0], dtype=jnp.int32)
    blocks = jnp.sum(
        jnp.where(page_table[None, :] == my_pages[:, None], block_ids[None, :], 0), axis=1
    )

    member = lax.axis_index("tensor")
    own_rows = row_count // lax.axis_size("tensor")
    own_stream = lax.dynamic_slice_in_dim(tokens, member * own_rows, own_rows, 0)
    own_ids = lax.dynamic_slice_in_dim(expert_ids, member * own_rows, own_rows, 0)
    hidden, key_cache, value_cache = attention(
        blocks,
        jnp.concatenate([key_rows, value_rows], axis=1),
        normed,
        query_weight,
        cosine,
        sine,
        (places - position)[:, None],
        out_weight,
        own_stream.astype(jnp.float32),
    )
    moe_input = rms_scale(hidden, expert_gain).astype(jnp.bfloat16)
    expert_count = router_weight.shape[1]
    probability = jax.nn.softmax(
        jnp.dot(moe_input, router_weight, preferred_element_type=jnp.float32), axis=-1
    )
    expert_range = jnp.arange(expert_count, dtype=jnp.int32)
    named = jnp.any(own_ids[:, :, None] == expert_range[None, None, :], axis=1)
    share = jnp.where(named, probability, 0.0)
    share_high = share.astype(jnp.bfloat16)
    share_low = (share - share_high.astype(jnp.float32)).astype(jnp.bfloat16)

    mine = jnp.concatenate([moe_input, share_high, share_low], axis=1)
    layer_out = mixture(mine, hidden, gate_weight, up_weight, down_weight)
    return (layer_out, key_cache, value_cache)


def solution(mesh):
    return jax.shard_map(
        local,
        mesh=mesh,
        in_specs=(
            P("seq", None),
            P(),
            P(),
            P(),
            P(None, "tensor"),
            P(None, "tensor"),
            P(None, "tensor"),
            P("tensor", None),
            P(),
            P(),
            P("seq", None),
            P("seq", None, "tensor"),
            P("seq", None, "tensor"),
            P("seq", "tensor", None),
        ),
        out_specs=(P("seq", None), P("seq", None, "tensor"), P("seq", None, "tensor")),
        check_vma=False,
    )
```
